32 devices in a mesh: rows: 8 (over z, y), sub: 4 (over x, core).
Axes of the slice: x: 2, y: 2, z: 4, core: 2. Of those that a mesh axis runs over, the one named last changes fastest.
Arguments:
- stiffness_tiles: bfloat16 [8, 4, 128, 128, 128], P('rows', 'sub'), may hold values from -0.5 to 0.5
- damping_tiles: bfloat16 [8, 4, 128, 128, 128], P('rows', 'sub'), may hold values from -0.5 to 0.5
- tile_map: int32 [8, 4, 2, 128], P('rows', 'sub'), may hold values from -1 to 767, as said below
- inv_mass: float32 [262144], P(('rows', 'sub')), may hold values from 0.5 to 2
- spectral_shift: float32 [], replicated, may hold values from 0.5 to 1.5
- basis: float32 [58, 262144], P(None, ('rows', 'sub')), may hold values from -20 to 20
- compact: float32 [2, 58, 57], replicated, may hold values from -0.54 to 0.54
Outputs:
- new_basis: float32 [2, 262144], P(None, ('rows', 'sub'))
- compact_out: float32 [2, 60, 59], replicated
- hessenberg: float32 [59, 2], replicated
The draws below stay inside these ranges and needn't reach their ends.
Inputs may be any that keep to these rules, and one draw needn't show every extreme that they name: tile_map[r, s, 0, t] is the tile row of part r that slot t adds to, or -1 for an unused slot; the used slots of a device come first, and some device uses all 128. tile_map[r, s, 1, t] is the source column tile counted from the start of part r - 1.
All inputs are finite; a program needn't handle non-finite values.
Results may differ from the reference program's by a relative error of at most 0.0033.
Values may be sent and summed in bfloat16 or wider, within the bound.
No kernel may reach another device: no remote copies, remote signals or barrier semaphores. Data moves between devices by JAX's collectives and lax.ppermute only.
A program may use at most 64 MiB of HBM per device.

```python
import math
import jax
import jax.numpy as jnp
from jax import lax

TILE = 128
RD = 8192
SLOTS = 128
K0 = 58
ITERS = 2
J0 = 57
NN = 262144
N_ROWS = 8
N_SUB = 4


def draw_tile_map(key, part):
    tile_rows = N_SUB * RD // TILE
    device_count = N_ROWS * N_SUB
    keys = jax.random.split(key, 5)
    light = SLOTS // 8 + jax.random.randint(keys[0], (device_count,), 0, 3 * SLOTS // 8 + 1)
    chosen = jax.random.randint(keys[1], (device_count,), 0, 8) == 0
    forced = jax.random.randint(keys[2], (), 0, device_count)
    heavy = jnp.logical_or(chosen, jnp.arange(device_count) == forced)
    live_count = jnp.where(heavy, SLOTS, light)
    target = jax.random.randint(keys[3], (device_count, SLOTS), 0, tile_rows)
    offset = jax.random.randint(keys[4], (device_count, SLOTS), -tile_rows, tile_rows + 1)
    source = tile_rows + target + offset
    used_slots = jnp.arange(SLOTS)[None, :] < live_count[:, None]
    target = jnp.where(used_slots, target, -1)
    stacked = jnp.stack([target, source], axis=1)
    return stacked.reshape(N_ROWS, N_SUB, 2, SLOTS).astype(jnp.int32)


def draw_basis(key, part):
    unknowns = RD * N_ROWS * N_SUB
    keys = jax.random.split(key, 1)
    position = jnp.arange(unknowns, dtype=jnp.float32) / unknowns
    scaling = math.sqrt(math.log(3.0) / 4.0) * jnp.exp(math.log(3.0) * position)
    values = jax.random.normal(keys[0], (K0, unknowns), jnp.float32) * scaling[None, :]
    return jnp.clip(values, -20.0, 20.0)


def steps_of(own_key, shape, pieces, low, high):
    loudness = 1.0
    for axis_at, blocks in pieces:
        draws = jax.random.uniform(jax.random.fold_in(jax.random.fold_in(own_key, 6), axis_at), (blocks,), jnp.float32, low / len(pieces), high / len(pieces))
        loudness = loudness * jnp.repeat(jnp.exp(draws), shape[axis_at] // blocks).reshape((-1,) + (1,) * (len(shape) - 1 - axis_at))
    return loudness


def bell_draw(stream_key, extent, width, bound, cuts=(), held_as=jnp.bfloat16):
    entries = width * jax.random.normal(stream_key, extent, jnp.float32)
    if cuts:
        entries = entries * steps_of(stream_key, extent, cuts, -0.22, 0.18)
    return jnp.clip(entries, -bound, bound).astype(held_as)


def setup_inputs(seed: int = 0) -> dict:
    splits = jax.random.split(jax.random.key(seed), 8)
    stiffness_tiles = bell_draw(splits[0], (N_ROWS, N_SUB, SLOTS, TILE, TILE), (SLOTS * TILE * TILE // (2 * RD)) ** -0.5, 0.5, ((0, 8), (1, 4)))
    damping_tiles = bell_draw(splits[1], (N_ROWS, N_SUB, SLOTS, TILE, TILE), (SLOTS * TILE * TILE // (2 * RD)) ** -0.5, 0.5, ((0, 8), (1, 4)))
    tile_map = draw_tile_map(jax.random.fold_in(splits[7], 71), 0)
    inv_mass = jnp.clip(jnp.exp(math.log(2.0) - 1.3862944 * jax.random.uniform(splits[3], (NN,), jnp.float32) ** steps_of(splits[3], (NN,), ((0, 32),), -0.2, 0.2)), 0.5, 2.0)
    spectral_shift = jnp.clip(jax.random.uniform(splits[4], (), jnp.float32, 0.5, 1.5), 0.5, 1.5)
    basis = draw_basis(jax.random.fold_in(splits[7], 71), 0)
    compact = bell_draw(splits[6], (2, K0, J0), 0.09, 0.54, (), jnp.float32)
    return dict(stiffness_tiles=stiffness_tiles, damping_tiles=damping_tiles, tile_map=tile_map, inv_mass=inv_mass, spectral_shift=spectral_shift, basis=basis, compact=compact)


precise = lax.Precision.HIGHEST

def coupled_products(stiffness_tiles, damping_tiles, tile_map, vectors):
    part_rows = N_SUB * RD
    tile_rows = part_rows // TILE
    padded = jnp.pad(vectors, ((0, 0), (part_rows, part_rows)))
    blocked = padded.reshape(2, -1, TILE)

    def one_part(part_index):
        damping = damping_tiles[part_index].reshape(N_SUB * SLOTS, TILE, TILE).astype(jnp.float32)
        stiffness = stiffness_tiles[part_index].reshape(N_SUB * SLOTS, TILE, TILE).astype(jnp.float32)
        target = tile_map[part_index, :, 0, :].reshape(-1)
        source = tile_map[part_index, :, 1, :].reshape(-1)
        window = lax.dynamic_slice_in_dim(blocked, part_index * tile_rows, 3 * tile_rows, 1).astype(jnp.float32)
        picked = window[:, source]
        product = jnp.einsum('sij,sj->si', damping, picked[0], precision=precise)
        product = product + jnp.einsum('sij,sj->si', stiffness, picked[1], precision=precise)
        usable = target >= 0
        product = jnp.where(usable[:, None], product, jnp.zeros_like(product))
        summed = jax.ops.segment_sum(product, jnp.where(usable, target, 0), num_segments=tile_rows)
        return summed.reshape(-1)
    parts_out = lax.map(one_part, jnp.arange(N_ROWS, dtype=jnp.int32))
    return parts_out.reshape(-1)

def compact_update(upper_half, lower_half, coefficients, norm_value, lower_tail):
    columns = upper_half.shape[1]
    zero_row = jnp.zeros((1, columns), upper_half.dtype)
    upper_ext = jnp.concatenate([upper_half, zero_row], 0)
    lower_ext = jnp.concatenate([lower_half, zero_row], 0)
    upper_coeffs = jnp.concatenate([coefficients, norm_value[None]])
    lower_coeffs = jnp.concatenate([lower_tail, jnp.zeros((1,), lower_tail.dtype)])
    weights = jnp.zeros((columns,), upper_half.dtype)
    for repeat_index in range(2):
        projection = jnp.dot(upper_coeffs, upper_ext, precision=precise) + jnp.dot(lower_coeffs, lower_ext, precision=precise)
        upper_coeffs = upper_coeffs - jnp.dot(upper_ext, projection, precision=precise)
        lower_coeffs = lower_coeffs - jnp.dot(lower_ext, projection, precision=precise)
        weights = weights + projection
    beta_norm = jnp.sqrt(jnp.sum(upper_coeffs * upper_coeffs) + jnp.sum(lower_coeffs * lower_coeffs) + 1e-06)
    upper_new = jnp.concatenate([upper_ext, (upper_coeffs / beta_norm)[:, None]], 1)
    lower_new = jnp.concatenate([lower_ext, (lower_coeffs / beta_norm)[:, None]], 1)
    return (upper_new, lower_new, weights, beta_norm)

def reference(stiffness_tiles, damping_tiles, tile_map, inv_mass, spectral_shift, basis, compact):
    unknowns = RD * N_ROWS * N_SUB
    held = basis
    upper_half = compact[0]
    lower_half = compact[1]
    new_columns = []
    hess_columns = []
    for iteration in range(ITERS):
        upper_last = upper_half[:, -1]
        lower_last = lower_half[:, -1]
        upper_vec = jnp.dot(upper_last, held, precision=precise)
        lower_vec = jnp.dot(lower_last, held, precision=precise)
        vectors = jnp.stack([upper_vec, lower_vec]).astype(jnp.bfloat16)
        coupled = coupled_products(stiffness_tiles, damping_tiles, tile_map, vectors)
        image = spectral_shift * upper_vec - inv_mass * coupled
        first_part = jnp.dot(held, image, precision=precise) / unknowns
        residual_one = image - jnp.dot(first_part, held, precision=precise)
        second_part = jnp.dot(held, residual_one, precision=precise) / unknowns
        residual_two = residual_one - jnp.dot(second_part, held, precision=precise)
        coefficients = first_part + second_part
        norm_value = jnp.sqrt(jnp.sum(residual_two * residual_two) / unknowns + 1e-06)
        column = residual_two / norm_value
        lower_tail = upper_last + spectral_shift * lower_last
        upper_half, lower_half, weights, beta_norm = compact_update(upper_half, lower_half, coefficients, norm_value, lower_tail)
        held = jnp.concatenate([held, column[None]], 0)
        new_columns.append(column)
        hess_columns.append(jnp.concatenate([weights, beta_norm[None], jnp.zeros((ITERS - 1 - iteration,), weights.dtype)]))
    return (jnp.stack(new_columns), jnp.stack([upper_half, lower_half]), jnp.stack(hess_columns, axis=1))
```

```python
import functools

import jax
import jax.numpy as jnp
from jax import lax
from jax.experimental import pallas as pl
from jax.experimental.pallas import tpu as pltpu
from jax.sharding import PartitionSpec as P

ITERS = 2
LANES = 128
SUBL = 8
F32 = jnp.float32
BF16 = jnp.bfloat16
VM = pltpu.VMEM
SM = pltpu.SMEM


def vmem():
    return pl.BlockSpec(memory_space=VM)


def smem():
    return pl.BlockSpec(memory_space=SM)


def iota(shape, axis):
    return lax.broadcasted_iota(jnp.int32, shape, axis)


def lane_sum(x):
    return jnp.sum(x, axis=1, keepdims=True)


def sub_sum(x):
    return jnp.sum(x, axis=0, keepdims=True)


def row_to_col(row, height):
    shape = (height, LANES)
    return lane_sum(jnp.where(iota(shape, 0) == iota(shape, 1), row, 0.0))


def col_to_row(col, height):
    shape = (height, LANES)
    return sub_sum(jnp.where(iota(shape, 0) == iota(shape, 1), col, 0.0))


def at_sublane(col, index):
    return jnp.sum(jnp.where(iota(col.shape, 0) == index, col, 0.0), axis=0, keepdims=True)


def gather_rows(parts):
    shift = 1
    while len(parts) > 1:
        low = (iota((SUBL, LANES), 0) // shift) % 2 == 0
        merged = []
        for a, b in zip(parts[0::2], parts[1::2]):
            moved = pltpu.roll(jnp.where(low, b, a), SUBL - shift, axis=0)
            merged.append(jnp.where(low, a, b) + moved)
        parts = merged
        shift *= 2
    return parts[0]


def block_rows(held_ref):
    n = held_ref.shape[0]
    return [(i, min(SUBL, n - i)) for i in range(0, n, SUBL)]


def combine(held_ref, cols, group):
    out = []
    totals = [[] for _ in cols]
    for k in range(SUBL):
        lanes = pl.ds((group * SUBL + k) * LANES, LANES)
        sums = [None] * len(cols)
        for start, size in block_rows(held_ref):
            block = held_ref[pl.ds(start, size), lanes]
            if size < SUBL:
                block = jnp.concatenate(
                    [block, jnp.zeros((SUBL - size, LANES), F32)], axis=0
                )
            for i, col in enumerate(cols):
                term = block * col[start : start + SUBL]
                sums[i] = term if sums[i] is None else sums[i] + term
        for i in range(len(cols)):
            totals[i].append(sums[i])
    for i in range(len(cols)):
        out.append(gather_rows(totals[i]))
    return out


def start_kernel(last_ref, held_ref, upper_ref, vec_ref):
    tiles = upper_ref.shape[0]
    n = held_ref.shape[0]
    height = -(-n // SUBL) * SUBL
    rows = jnp.pad(last_ref[...], ((0, 0), (0, LANES - n)))
    cols = [
        jnp.broadcast_to(row_to_col(rows[i : i + 1], height), (height, LANES)) for i in range(2)
    ]
    for group in range(tiles // SUBL):
        upper, lower = combine(held_ref, cols, group)
        at = group * SUBL
        upper_ref[at : at + SUBL] = upper
        vec_ref[at : at + SUBL] = upper.astype(BF16)
        vec_ref[tiles + at : tiles + at + SUBL] = lower.astype(BF16)


def tile_kernel(
    rows_count,
    sub_count,
    packed,
    map_ref,
    target_ref,
    pair_ref,
    mine_ref,
    other_ref,
    damping_ref,
    stiffness_ref,
    *rest,
):
    if packed:
        gram_ref, rest = rest[0], rest[1:]
    outs, rest = rest[:sub_count], rest[sub_count:]
    window_ref, picked_ref, product_ref = rest[:3]
    step = pl.program_id(0)
    r = lax.axis_index("rows")
    s = lax.axis_index("sub")
    tiles = pair_ref.shape[1] // 2
    slots = product_ref.shape[0]
    block = damping_ref.shape[0]
    part_tiles = sub_count * tiles

    @pl.when(step == 0)
    def _():
        def put(value, part, sub, scale):
            at = pl.multiple_of((part * sub_count + sub) * tiles, tiles)
            wide = value.astype(F32)
            if scale is not None:
                wide = wide * scale
            window_ref[0, pl.ds(at, tiles)] = wide[:tiles]
            window_ref[1, pl.ds(at, tiles)] = wide[tiles:]

        put(pair_ref[0], 1, s, None)
        put(pair_ref[1], 1, s ^ 1, None)
        towards = jnp.where((r + s) % 2 == 0, 1, -1)
        half = sub_count // 2
        for source_ref, base, rel in ((mine_ref, s, towards), (other_ref, s ^ 1, -towards)):
            for k in range(1, half):
                put(source_ref[k - 1], 1, base ^ (2 * k), None)
            inside = jnp.logical_and(r + rel >= 0, r + rel < rows_count)
            scale = jnp.where(inside, 1.0, 0.0)
            for k in range(half):
                for e in range(2):
                    put(
                        source_ref[half - 1 + 2 * k + e],
                        1 + rel,
                        base ^ (2 * k) ^ e,
                        scale,
                    )
        for t in range(slots):
            source = jnp.clip(map_ref[1, t], 0, 3 * part_tiles - 1)
            picked_ref[0, t : t + 1] = window_ref[0, pl.ds(source, 1)]
            picked_ref[1, t : t + 1] = window_ref[1, pl.ds(source, 1)]

    at = pl.ds(pl.multiple_of(step * block, block), block)
    dims = (((1,), (1,)), ((), ()))
    result = lax.dot_general(
        picked_ref[0, at].astype(BF16),
        damping_ref[...].reshape(block * LANES, LANES),
        dims,
        preferred_element_type=F32,
    ) + lax.dot_general(
        picked_ref[1, at].astype(BF16),
        stiffness_ref[...].reshape(block * LANES, LANES),
        dims,
        preferred_element_type=F32,
    )
    own = jnp.zeros((block, LANES), F32)
    for t in range(block):
        own = own + jnp.where(
            iota((block, LANES), 0) == t, result[:, t * LANES : (t + 1) * LANES], 0.0
        )
    product_ref[at] = own

    @pl.when(step == pl.num_programs(0) - 1)
    def _():
        target = target_ref[...]
        target = jnp.where(target >= 0, target ^ (s * tiles), -1)
        selector = jnp.where(iota((part_tiles, slots), 0) == target, 1.0, 0.0).astype(BF16)
        left = product_ref[...]
        summed = jnp.zeros((part_tiles, LANES), F32)
        for _ in range(3):
            piece = left.astype(BF16)
            summed = summed + jnp.dot(selector, piece, preferred_element_type=F32)
            left = left - piece.astype(F32)
        for k in range(sub_count):
            outs[k][:tiles] = summed[k * tiles : (k + 1) * tiles]
        if packed:
            square_ref = rest[3]
            n = gram_ref.shape[0]
            square_ref[...] = jnp.zeros(square_ref.shape, F32)
            square_ref[:n, :n] = gram_ref[...]
            share = square_ref.shape[0] // sub_count
            for k in range(sub_count):
                start = pl.multiple_of((s ^ k) * share, SUBL)
                low = square_ref[pl.ds(start, SUBL)]
                high = square_ref[pl.ds(start + SUBL, SUBL)]
                outs[k][tiles:] = low + pltpu.roll(high, LANES // 2, axis=1)


def inner_kernel(sub_count, packed, shift_ref, *refs):
    parts = refs[:sub_count]
    upper_ref, mass_ref, held_ref = refs[sub_count : sub_count + 3]
    refs = refs[sub_count + 3 :]
    if not packed:
        column_ref, refs = refs[0], refs[1:]
    image_ref, packet_ref = refs
    tiles = upper_ref.shape[0]
    n = held_ref.shape[0]
    total = parts[0][:tiles]
    for k in range(1, sub_count):
        total = total + parts[k][:tiles]
    image = shift_ref[0] * upper_ref[...] - mass_ref[...] * total
    image_ref[...] = image
    square = lane_sum(sub_sum(image * image))
    blocks = block_rows(held_ref)
    sums = [None] * len(blocks)
    for k in range(tiles):
        row = image_ref[k : k + 1]
        for i, (start, size) in enumerate(blocks):
            term = held_ref[pl.ds(start, size), pl.ds(k * LANES, LANES)] * row
            sums[i] = term if sums[i] is None else sums[i] + term
    cols = []
    for total_block, (start, size) in zip(sums, blocks):
        col = lane_sum(total_block)
        if size < SUBL:
            col = jnp.concatenate([col, jnp.zeros((SUBL - size, 1), F32)], axis=0)
        cols.append(col)
    lane = iota((SUBL, LANES), 1)
    if packed:
        packet = parts[0][tiles:]
        for k in range(1, sub_count):
            packet = packet + parts[k][tiles:]
        for i, col in enumerate(cols):
            spot = (i % 2) * (LANES // 2) + n + i // 2
            packet = jnp.where(lane == spot, col, packet)
        spot = n + (len(cols) + 1) // 2
        first = iota((SUBL, LANES), 0) == 0
        packet = jnp.where(jnp.logical_and(lane == spot, first), square, packet)
        packet_ref[...] = jnp.broadcast_to(packet[None], packet_ref.shape)
    else:
        height = SUBL * len(cols)
        row = col_to_row(jnp.concatenate(cols, axis=0), height)
        extra = lane_sum(sub_sum(image * column_ref[...]))
        row = jnp.where(lane[:1] == n, extra, row)
        row = jnp.where(lane[:1] == LANES - 1, square, row)
        packet_ref[...] = jnp.broadcast_to(row[None], packet_ref.shape)


def update_kernel(unknowns, sub_count, iteration, last, shift_ref, *refs):
    packet_ref, image_ref, held_ref, upper_half_ref, lower_half_ref = refs[:5]
    refs = refs[5:]
    n0 = held_ref.shape[0]
    n = n0 + iteration
    tiles = image_ref.shape[0]
    height = -(-n0 // (2 * SUBL)) * 2 * SUBL
    shape = (height, LANES)
    lane = iota(shape, 1)
    subl = iota(shape, 0)
    inverse = 1.0 / unknowns
    if iteration == 0:
        out_refs = refs
        count = packet_ref.shape[0] // sub_count
        blocks = []
        for s in range(sub_count):
            total = packet_ref[s]
            for r in range(1, count):
                total = total + packet_ref[r * sub_count + s]
            blocks.append(total)
        every = blocks[0]
        for s in range(1, sub_count):
            every = every + blocks[s]
        lane8 = iota((SUBL, LANES), 1)
        gram = []
        for total in blocks:
            gram.append(jnp.where(lane8 < n, total, 0.0))
            gram.append(jnp.where(lane8 < n, pltpu.roll(total, LANES // 2, axis=1), 0.0))
        gram = jnp.concatenate(gram, axis=0) * inverse
        pieces = -(-n0 // SUBL)
        cols = []
        for i in range(height // SUBL):
            spot = (i % 2) * (LANES // 2) + n + i // 2
            cols.append(lane_sum(jnp.where(lane8 == spot, every, 0.0)))
        first_col = jnp.concatenate(cols, axis=0) * inverse
        first_row = col_to_row(first_col, height)
        spot = n + (pieces + 1) // 2
        self_mean = sub_sum(lane_sum(jnp.where(lane8 == spot, every, 0.0))) * inverse
    else:
        gram_ref, column_ref, weights_ref = refs[:3]
        out_refs = refs[3:]
        total = packet_ref[0]
        for i in range(1, packet_ref.shape[0]):
            total = total + packet_ref[i]
        gram = gram_ref[...]
        first_row = jnp.where(lane[:1] < n, total, 0.0) * inverse
        first_col = row_to_col(first_row, height)
        self_mean = lane_sum(jnp.where(lane[:1] == LANES - 1, total, 0.0)) * inverse
    coef_col = first_col + (first_col - lane_sum(gram * first_row))
    coef_row = first_row + (first_row - sub_sum(gram * first_col))
    gram_coef = lane_sum(gram * coef_row)
    mean_square = self_mean - 2.0 * sub_sum(coef_col * first_col) + sub_sum(coef_col * gram_coef)
    norm = jnp.sqrt(mean_square + 1e-06)
    upper_half = upper_half_ref[...]
    lower_half = lower_half_ref[...]
    columns = n - 1
    shift = shift_ref[0]
    tail = lane_sum(jnp.where(lane == columns - 1, upper_half + shift * lower_half, 0.0))
    upper_coef = jnp.where(subl[:, :1] == n, norm, coef_col)
    lower_coef = tail
    weights = jnp.zeros((1, LANES), F32)
    for _ in range(2):
        projection = sub_sum(upper_half * upper_coef + lower_half * lower_coef)
        upper_coef = upper_coef - lane_sum(upper_half * projection)
        lower_coef = lower_coef - lane_sum(lower_half * projection)
        weights = weights + projection
    beta = jnp.sqrt(sub_sum(upper_coef * upper_coef + lower_coef * lower_coef) + 1e-06)
    upper_new = upper_coef / beta
    lower_new = lower_coef / beta
    upper_half = jnp.where(lane == columns, upper_new, upper_half)
    lower_half = jnp.where(lane == columns, lower_new, lower_half)
    weights = jnp.where(lane[:1] == columns, beta, weights)
    coef_wide = jnp.broadcast_to(coef_col, shape)
    if not last:
        column_ref, upper_ref, vec_ref, upper_half_out, lower_half_out, gram_out, weights_out = (
            out_refs
        )
        upper_half_out[...] = upper_half
        lower_half_out[...] = lower_half
        weights_out[...] = jnp.broadcast_to(weights, (SUBL, LANES))
        cross_col = (first_col - gram_coef) / norm
        cross_row = (first_row - sub_sum(gram * coef_col)) / norm
        gram = jnp.where(lane == n, cross_col, gram)
        gram = jnp.where(subl == n, cross_row, gram)
        corner = jnp.logical_and(lane == n, subl == n)
        gram_out[...] = jnp.where(corner, mean_square / (norm * norm), gram)
        upper_wide = jnp.broadcast_to(upper_new, shape)
        lower_wide = jnp.broadcast_to(lower_new, shape)
        upper_last = at_sublane(upper_new, n)
        lower_last = at_sublane(lower_new, n)
        for group in range(tiles // SUBL):
            at = group * SUBL
            along, upper, lower = combine(held_ref, [coef_wide, upper_wide, lower_wide], group)
            column = (image_ref[at : at + SUBL] - along) / norm
            upper = upper + column * upper_last
            lower = lower + column * lower_last
            column_ref[at : at + SUBL] = column
            upper_ref[at : at + SUBL] = upper
            vec_ref[at : at + SUBL] = upper.astype(BF16)
            vec_ref[tiles + at : tiles + at + SUBL] = lower.astype(BF16)
    else:
        basis_ref, compact_ref, hess_ref = out_refs
        compact_ref[0] = upper_half[: n + 1, :n]
        compact_ref[1] = lower_half[: n + 1, :n]
        hess = jnp.where(
            lane == 0,
            row_to_col(weights_ref[:1], height),
            row_to_col(weights, height),
        )
        hess_ref[...] = hess[:n, :2]
        coef_last = at_sublane(coef_col, n0)
        for group in range(tiles // SUBL):
            at = group * SUBL
            (along,) = combine(held_ref, [coef_wide], group)
            before = column_ref[at : at + SUBL]
            column = (image_ref[at : at + SUBL] - along - before * coef_last) / norm
            for k in range(SUBL):
                lanes = pl.ds((at + k) * LANES, LANES)
                basis_ref[0:1, lanes] = before[k : k + 1]
                basis_ref[1:2, lanes] = column[k : k + 1]


def call(body, outs, args, specs, scratch=(), grid=None):
    arguments = dict(
        out_shape=[jax.ShapeDtypeStruct(shape, dtype) for shape, dtype in outs],
        in_specs=specs,
        out_specs=[vmem()] * len(outs),
        scratch_shapes=list(scratch),
    )
    if grid is not None:
        arguments.update(
            grid=grid,
            out_specs=[
                pl.BlockSpec(shape, lambda i, rank=len(shape): (0,) * rank) for shape, _ in outs
            ],
        )
    return pl.pallas_call(body, **arguments)(*args)


def on_device(stiffness_tiles, damping_tiles, tile_map, inv_mass, spectral_shift, basis, compact):
    rows_count = lax.axis_size("rows")
    sub_count = lax.axis_size("sub")
    devices = rows_count * sub_count
    half = sub_count // 2
    tile_size = stiffness_tiles.shape[-1]
    slots = stiffness_tiles.shape[2]
    held_count, local_rows = basis.shape
    tiles = local_rows // tile_size
    unknowns = local_rows * devices
    height = -(-held_count // (2 * SUBL)) * 2 * SUBL
    block = 2 * SUBL
    every = ("rows", "sub")

    def swap(value, partner):
        pairs = []
        for r in range(rows_count):
            for s in range(sub_count):
                to_r, to_s = partner(r, s)
                pairs.append((r * sub_count + s, to_r * sub_count + to_s))
        return lax.ppermute(value, every, pairs)

    def beside(r, s):
        return r ^ 1 if s % 2 == 0 else (((r + 1) ^ 1) - 1) % rows_count

    slot_map = tile_map[0, 0]
    damping = damping_tiles[0, 0]
    stiffness = stiffness_tiles[0, 0]
    shift = spectral_shift.reshape(1)
    mass = inv_mass.reshape(tiles, tile_size)
    field = ((tiles, tile_size), F32)
    vector = ((2 * tiles, tile_size), BF16)
    square = ((height, LANES), F32)

    upper_vec, vectors = call(
        start_kernel, [field, vector], (compact[:, :, -1], basis), [vmem(), vmem()]
    )
    padding = ((0, 0), (0, height - compact.shape[1]), (0, LANES - compact.shape[2]))
    halves = jnp.pad(compact, padding)
    upper_half, lower_half = halves[0], halves[1]
    gram = jnp.dot(basis, basis.T, precision=lax.Precision.HIGHEST)
    column = weights = None
    for iteration in range(ITERS):
        packed = iteration == 0
        last = iteration == ITERS - 1
        pair = jnp.stack([vectors, swap(vectors, lambda r, s: (r, s ^ 1))])
        mine = [
            swap(vectors, lambda r, s, k=k: (r, s ^ (2 * k)))[None] for k in range(1, half)
        ] + [swap(pair, lambda r, s, k=k: (beside(r, s), s ^ (2 * k))) for k in range(half)]
        mine = jnp.concatenate(mine, axis=0)
        other = swap(mine, lambda r, s: (r, s ^ 1))
        depth = tiles + SUBL if packed else tiles
        full = lambda shape: pl.BlockSpec(shape, lambda i, rank=len(shape): (0,) * rank)
        tile_spec = pl.BlockSpec((block, tile_size, tile_size), lambda i: (i, 0, 0))
        scratch = [
            pltpu.VMEM((2, 3 * sub_count * tiles, LANES), F32),
            pltpu.VMEM((2, slots, LANES), F32),
            pltpu.VMEM((slots, LANES), F32),
        ]
        args = [slot_map, slot_map[:1], pair, mine, other, damping, stiffness]
        specs = [
            smem(),
            full((1, slots)),
            full(pair.shape),
            full(mine.shape),
            full(other.shape),
            tile_spec,
            tile_spec,
        ]
        if packed:
            args.append(gram)
            specs.append(full(gram.shape))
            scratch.append(pltpu.VMEM((height, LANES), F32))
        parts = call(
            functools.partial(tile_kernel, rows_count, sub_count, packed),
            [((depth, LANES), F32)] * sub_count,
            args,
            specs,
            scratch,
            grid=(slots // block,),
        )
        parts = [parts[0]] + [
            swap(parts[k], lambda r, s, k=k: (r, s ^ k)) for k in range(1, sub_count)
        ]
        packet = (devices, SUBL, LANES) if packed else (devices, 1, LANES)
        args = [shift, *parts, upper_vec, mass, basis]
        if not packed:
            args.append(column)
        image, sent = call(
            functools.partial(inner_kernel, sub_count, packed),
            [field, (packet, F32)],
            args,
            [smem()] + [vmem()] * (len(args) - 1),
        )
        received = lax.all_to_all(sent, every, 0, 0)
        args = [shift, received, image, basis, upper_half, lower_half]
        if not packed:
            args += [gram, column, weights]
        if last:
            total = held_count + ITERS
            outs = [
                ((ITERS, local_rows), F32),
                ((2, total, total - 1), F32),
                ((total - 1, ITERS), F32),
            ]
        else:
            outs = [field, field, vector, square, square, square, ((SUBL, LANES), F32)]
        outs = call(
            functools.partial(update_kernel, unknowns, sub_count, iteration, last),
            outs,
            args,
            [smem()] + [vmem()] * (len(args) - 1),
        )
        if not last:
            column, upper_vec, vectors, upper_half, lower_half, gram, weights = outs
    return tuple(outs)


def solution(mesh):
    in_specs = (
        P("rows", "sub", None, None, None),
        P("rows", "sub", None, None, None),
        P("rows", "sub", None, None),
        P(("rows", "sub")),
        P(),
        P(None, ("rows", "sub")),
        P(),
    )
    out_specs = (P(None, ("rows", "sub")), P(), P())
    return jax.shard_map(
        on_device, mesh=mesh, in_specs=in_specs, out_specs=out_specs, check_vma=False
    )
```

```python
import functools

import jax
import jax.numpy as jnp
from jax import lax
from jax.experimental import pallas as pl
from jax.experimental.pallas import tpu as pltpu
from jax.sharding import PartitionSpec as P

ITERS = 2
LANES = 128
SUBL = 8
F32 = jnp.float32
BF16 = jnp.bfloat16
VM = pltpu.VMEM
SM = pltpu.SMEM
GRANT = 24 * 1024 * 1024


def iota(shape, axis):
    return lax.broadcasted_iota(jnp.int32, shape, axis)


def lane_sum(x):
    return jnp.sum(x, axis=1, keepdims=True)


def sub_sum(x):
    return jnp.sum(x, axis=0, keepdims=True)


def row_to_col(row, height):
    shape = (height, LANES)
    return lane_sum(jnp.where(iota(shape, 0) == iota(shape, 1), row, 0.0))


def col_to_row(col, height):
    shape = (height, LANES)
    return sub_sum(jnp.where(iota(shape, 0) == iota(shape, 1), col, 0.0))


def at_sublane(col, index):
    return jnp.sum(jnp.where(iota(col.shape, 0) == index, col, 0.0), axis=0, keepdims=True)


def gather_rows(parts):
    shift = 1
    while len(parts) > 1:
        low = (iota((SUBL, LANES), 0) // shift) % 2 == 0
        merged = []
        for a, b in zip(parts[0::2], parts[1::2]):
            moved = pltpu.roll(jnp.where(low, b, a), SUBL - shift, axis=0)
            merged.append(jnp.where(low, a, b) + moved)
        parts = merged
        shift *= 2
    return parts[0]


def block_rows(held_ref):
    n = held_ref.shape[0]
    return [(i, min(SUBL, n - i)) for i in range(0, n, SUBL)]


def combine(held_ref, cols, group):
    out = []
    totals = [[] for _ in cols]
    for k in range(SUBL):
        lanes = pl.ds((group * SUBL + k) * LANES, LANES)
        sums = [None] * len(cols)
        for start, size in block_rows(held_ref):
            block = held_ref[pl.ds(start, size), lanes]
            if size < SUBL:
                block = jnp.concatenate(
                    [block, jnp.zeros((SUBL - size, LANES), F32)], axis=0
                )
            for i, col in enumerate(cols):
                term = block * col[start : start + SUBL]
                sums[i] = term if sums[i] is None else sums[i] + term
        for i in range(len(cols)):
            totals[i].append(sums[i])
    for i in range(len(cols)):
        out.append(gather_rows(totals[i]))
    return out


def start_kernel(compact_ref, basis_ref, upper_ref, vec_ref, held_ref, last_ref, sems):
    tiles = upper_ref.shape[0]
    n = held_ref.shape[0]
    groups = tiles // SUBL
    height = -(-n // SUBL) * SUBL
    span = SUBL * LANES
    first = pltpu.make_async_copy(
        compact_ref.at[compact_ref.shape[0] - 1], last_ref, sems.at[groups]
    )
    first.start()
    copies = []
    for group in range(groups):
        lanes = pl.ds(group * span, span)
        copies.append(
            pltpu.make_async_copy(basis_ref.at[:, lanes], held_ref.at[:, lanes], sems.at[group])
        )
        copies[-1].start()
    first.wait()
    rows = jnp.pad(last_ref[...], ((0, 0), (0, LANES - n)))
    cols = [
        jnp.broadcast_to(row_to_col(rows[i : i + 1], height), (height, LANES)) for i in range(2)
    ]
    for group in range(groups):
        copies[group].wait()
        upper, lower = combine(held_ref, cols, group)
        at = group * SUBL
        upper_ref[at : at + SUBL] = upper
        vec_ref[at : at + SUBL] = upper.astype(BF16)
        vec_ref[tiles + at : tiles + at + SUBL] = lower.astype(BF16)


def tile_kernel(
    block,
    sub_count,
    packed,
    source_ref,
    target_ref,
    quarter_ref,
    pair_ref,
    mine_ref,
    other_ref,
    damping_ref,
    stiffness_ref,
    *rest,
):
    if packed:
        gram_ref, rest = rest[0], rest[1:]
    outs, rest = rest[:sub_count], rest[sub_count:]
    picked_ref, product_ref, buffer_ref, sems = rest[:4]
    tiles = pair_ref.shape[1] // 2
    slots = damping_ref.shape[0]
    part_tiles = sub_count * tiles

    copies = []
    for step in range(slots // block):
        at = pl.ds(step * block, block)
        for i, ref in enumerate((damping_ref, stiffness_ref)):
            copies.append(
                pltpu.make_async_copy(ref.at[at], buffer_ref.at[i, at], sems.at[i, step])
            )
            copies[-1].start()

    window = []
    for ref in (pair_ref, mine_ref, other_ref):
        for i in range(ref.shape[0]):
            window.append(jnp.concatenate([ref[i, :tiles], ref[i, tiles:]], axis=1))
    window = jnp.concatenate(window, axis=0)
    depth = window.shape[0]
    chooser = jnp.where(iota((slots, depth), 1) == source_ref[...], 1.0, 0.0).astype(BF16)
    picked_ref[...] = jnp.dot(chooser, window, preferred_element_type=F32).astype(BF16)

    dims = (((1,), (1,)), ((), ()))
    for step in range(slots // block):
        at = pl.ds(step * block, block)
        copies[2 * step].wait()
        copies[2 * step + 1].wait()
        both = jnp.concatenate(
            [buffer_ref[i, at].reshape(block * LANES, LANES) for i in range(2)], axis=1
        )
        result = lax.dot_general(picked_ref[at], both, dims, preferred_element_type=F32)
        own = jnp.zeros((block, LANES), F32)
        for t in range(block):
            own = jnp.where(
                iota((block, LANES), 0) == t, result[:, t * LANES : (t + 1) * LANES], own
            )
        product_ref[at] = own

    selector = jnp.where(iota((part_tiles, slots), 0) == target_ref[...], 1.0, 0.0).astype(BF16)
    left = product_ref[...]
    summed = jnp.zeros((part_tiles, LANES), F32)
    for _ in range(3):
        piece = left.astype(BF16)
        summed = summed + jnp.dot(selector, piece, preferred_element_type=F32)
        left = left - piece.astype(F32)
    for k in range(sub_count):
        outs[k][:tiles] = summed[k * tiles : (k + 1) * tiles]
    if packed:
        square_ref = rest[4]
        n = gram_ref.shape[0]
        square_ref[...] = jnp.zeros(square_ref.shape, F32)
        square_ref[:n, :n] = gram_ref[...]
        share = square_ref.shape[0] // sub_count
        for k in range(sub_count):
            start = pl.multiple_of((quarter_ref[0] ^ k) * share, SUBL)
            low = square_ref[pl.ds(start, SUBL)]
            high = square_ref[pl.ds(start + SUBL, SUBL)]
            outs[k][tiles:] = low + pltpu.roll(high, LANES // 2, axis=1)


def inner_kernel(sub_count, packed, shift_ref, *refs):
    parts = refs[:sub_count]
    upper_ref, mass_ref, held_ref = refs[sub_count : sub_count + 3]
    refs = refs[sub_count + 3 :]
    if not packed:
        column_ref, refs = refs[0], refs[1:]
    image_ref, packet_ref = refs
    tiles = upper_ref.shape[0]
    n = held_ref.shape[0]
    total = parts[0][:tiles]
    for k in range(1, sub_count):
        total = total + parts[k][:tiles]
    image = shift_ref[0] * upper_ref[...] - mass_ref[...] * total
    image_ref[...] = image
    square = lane_sum(sub_sum(image * image))
    blocks = block_rows(held_ref)
    sums = [None] * len(blocks)
    for k in range(tiles):
        row = image_ref[k : k + 1]
        for i, (start, size) in enumerate(blocks):
            term = held_ref[pl.ds(start, size), pl.ds(k * LANES, LANES)] * row
            sums[i] = term if sums[i] is None else sums[i] + term
    cols = []
    for total_block, (start, size) in zip(sums, blocks):
        col = lane_sum(total_block)
        if size < SUBL:
            col = jnp.concatenate([col, jnp.zeros((SUBL - size, 1), F32)], axis=0)
        cols.append(col)
    lane = iota((SUBL, LANES), 1)
    if packed:
        packet = parts[0][tiles:]
        for k in range(1, sub_count):
            packet = packet + parts[k][tiles:]
        for i, col in enumerate(cols):
            spot = (i % 2) * (LANES // 2) + n + i // 2
            packet = jnp.where(lane == spot, col, packet)
        spot = n + (len(cols) + 1) // 2
        first = iota((SUBL, LANES), 0) == 0
        packet = jnp.where(jnp.logical_and(lane == spot, first), square, packet)
        packet_ref[...] = jnp.broadcast_to(packet[None], packet_ref.shape)
    else:
        height = SUBL * len(cols)
        row = col_to_row(jnp.concatenate(cols, axis=0), height)
        extra = lane_sum(sub_sum(image * column_ref[...]))
        row = jnp.where(lane[:1] == n, extra, row)
        row = jnp.where(lane[:1] == LANES - 1, square, row)
        packet_ref[...] = jnp.broadcast_to(row[None], packet_ref.shape)


def update_kernel(unknowns, sub_count, iteration, last, shift_ref, *refs):
    packet_ref, image_ref, held_ref, upper_half_ref, lower_half_ref = refs[:5]
    refs = refs[5:]
    n0 = held_ref.shape[0]
    n = n0 + iteration
    tiles = image_ref.shape[0]
    height = -(-n0 // (2 * SUBL)) * 2 * SUBL
    shape = (height, LANES)
    lane = iota(shape, 1)
    subl = iota(shape, 0)
    inverse = 1.0 / unknowns
    if iteration == 0:
        out_refs = refs
        count = packet_ref.shape[0] // sub_count
        blocks = []
        for s in range(sub_count):
            total = packet_ref[s]
            for r in range(1, count):
                total = total + packet_ref[r * sub_count + s]
            blocks.append(total)
        every = blocks[0]
        for s in range(1, sub_count):
            every = every + blocks[s]
        lane8 = iota((SUBL, LANES), 1)
        gram = []
        for total in blocks:
            gram.append(jnp.where(lane8 < n, total, 0.0))
            gram.append(jnp.where(lane8 < n, pltpu.roll(total, LANES // 2, axis=1), 0.0))
        gram = jnp.concatenate(gram, axis=0) * inverse
        pieces = -(-n0 // SUBL)
        cols = []
        for i in range(height // SUBL):
            spot = (i % 2) * (LANES // 2) + n + i // 2
            cols.append(lane_sum(jnp.where(lane8 == spot, every, 0.0)))
        first_col = jnp.concatenate(cols, axis=0) * inverse
        first_row = col_to_row(first_col, height)
        spot = n + (pieces + 1) // 2
        self_mean = sub_sum(lane_sum(jnp.where(lane8 == spot, every, 0.0))) * inverse
    else:
        gram_ref, column_ref, weights_ref = refs[:3]
        out_refs = refs[5:]
        total = packet_ref[0]
        for i in range(1, packet_ref.shape[0]):
            total = total + packet_ref[i]
        gram = gram_ref[...]
        first_row = jnp.where(lane[:1] < n, total, 0.0) * inverse
        first_col = row_to_col(first_row, height)
        self_mean = lane_sum(jnp.where(lane[:1] == LANES - 1, total, 0.0)) * inverse
    coef_col = first_col + (first_col - lane_sum(gram * first_row))
    coef_row = first_row + (first_row - sub_sum(gram * first_col))
    gram_coef = lane_sum(gram * coef_row)
    mean_square = self_mean - 2.0 * sub_sum(coef_col * first_col) + sub_sum(coef_col * gram_coef)
    norm = jnp.sqrt(mean_square + 1e-06)
    upper_half = upper_half_ref[...]
    lower_half = lower_half_ref[...]
    columns = n - 1
    shift = shift_ref[0]
    tail = lane_sum(jnp.where(lane == columns - 1, upper_half + shift * lower_half, 0.0))
    upper_coef = jnp.where(subl[:, :1] == n, norm, coef_col)
    lower_coef = tail
    weights = jnp.zeros((1, LANES), F32)
    for _ in range(2):
        projection = sub_sum(upper_half * upper_coef + lower_half * lower_coef)
        upper_coef = upper_coef - lane_sum(upper_half * projection)
        lower_coef = lower_coef - lane_sum(lower_half * projection)
        weights = weights + projection
    beta = jnp.sqrt(sub_sum(upper_coef * upper_coef + lower_coef * lower_coef) + 1e-06)
    upper_new = upper_coef / beta
    lower_new = lower_coef / beta
    upper_half = jnp.where(lane == columns, upper_new, upper_half)
    lower_half = jnp.where(lane == columns, lower_new, lower_half)
    weights = jnp.where(lane[:1] == columns, beta, weights)
    coef_wide = jnp.broadcast_to(coef_col, shape)
    if not last:
        column_ref, upper_ref, vec_ref = out_refs[:3]
        upper_half_out, lower_half_out, gram_out, weights_out, added_ref = out_refs[3:]
        added_ref[0, 0:1] = col_to_row(upper_new, height)
        added_ref[0, 1:2] = col_to_row(lower_new, height)
        upper_half_out[...] = upper_half
        lower_half_out[...] = lower_half
        weights_out[...] = jnp.broadcast_to(weights, (SUBL, LANES))
        cross_col = (first_col - gram_coef) / norm
        cross_row = (first_row - sub_sum(gram * coef_col)) / norm
        gram = jnp.where(lane == n, cross_col, gram)
        gram = jnp.where(subl == n, cross_row, gram)
        corner = jnp.logical_and(lane == n, subl == n)
        gram_out[...] = jnp.where(corner, mean_square / (norm * norm), gram)
        upper_wide = jnp.broadcast_to(upper_new, shape)
        lower_wide = jnp.broadcast_to(lower_new, shape)
        upper_last = at_sublane(upper_new, n)
        lower_last = at_sublane(lower_new, n)
        for group in range(tiles // SUBL):
            at = group * SUBL
            along, upper, lower = combine(held_ref, [coef_wide, upper_wide, lower_wide], group)
            column = (image_ref[at : at + SUBL] - along) / norm
            upper = upper + column * upper_last
            lower = lower + column * lower_last
            column_ref[at : at + SUBL] = column
            upper_ref[at : at + SUBL] = upper
            vec_ref[at : at + SUBL] = upper.astype(BF16)
            vec_ref[tiles + at : tiles + at + SUBL] = lower.astype(BF16)
    else:
        basis_ref, compact_ref, hess_ref = out_refs
        before_ref, first_ref = refs[3:5]
        out_refs = None
        old, pair, width = before_ref.shape
        compact_ref[:old, :, :width] = before_ref[...]
        compact_ref[:old, :, width:] = jnp.zeros((old, pair, n + 1 - width), F32)
        compact_ref[old : old + 1] = first_ref[:, :, : n + 1]
        compact_ref[old + 1, 0:1] = col_to_row(upper_new, height)[:, : n + 1]
        compact_ref[old + 1, 1:2] = col_to_row(lower_new, height)[:, : n + 1]
        hess_ref[0:1] = weights_ref[:1, :n]
        hess_ref[1:2] = weights[:, :n]
        coef_last = at_sublane(coef_col, n0)
        for group in range(tiles // SUBL):
            at = group * SUBL
            (along,) = combine(held_ref, [coef_wide], group)
            before = column_ref[at : at + SUBL]
            column = (image_ref[at : at + SUBL] - along - before * coef_last) / norm
            for k in range(SUBL):
                lanes = pl.ds((at + k) * LANES, LANES)
                basis_ref[0:1, lanes] = before[k : k + 1]
                basis_ref[1:2, lanes] = column[k : k + 1]


def call(body, outs, args, scratch=(), final=False, far=()):
    specs, values = [], []
    for i, value in enumerate(args):
        space = pltpu.HBM if i in far else SM if value.shape == (1,) else VM
        specs.append(pl.BlockSpec(memory_space=space))
        values.append(
            value if space == SM else pltpu.with_memory_space_constraint(value, space)
        )
    return pl.pallas_call(
        body,
        out_shape=[
            jax.ShapeDtypeStruct(shape, dtype) if final else VM(shape, dtype)
            for shape, dtype in outs
        ],
        in_specs=specs,
        out_specs=[pl.BlockSpec(memory_space=VM)] * len(outs),
        scratch_shapes=list(scratch),
        compiler_params=pltpu.CompilerParams(vmem_limit_bytes=GRANT),
    )(*values)


def window_rows(slot_map, rows_count, sub_count, tiles):
    r = lax.axis_index("rows")
    s = lax.axis_index("sub")
    half = sub_count // 2
    mine = 2
    other = mine + half - 1 + sub_count
    source = slot_map[1]
    part = source // (sub_count * tiles) - 1
    sub = (source // tiles) % sub_count
    beside = (sub ^ s) & 1
    same = sub ^ s
    within = jnp.where(
        same < 2, same, jnp.where(beside == 0, mine, other) + (same >> 1) - 1
    )
    towards = jnp.where((r + s) % 2 == 0, 1, -1)
    away = half - 1 + jnp.where(part == towards, mine + same, other + (same ^ 1))
    slice_at = jnp.where(part == 0, within, away)
    inside = (r + part >= 0) & (r + part < rows_count)
    row = jnp.where(inside, slice_at * tiles + source % tiles, -1)
    target = jnp.where(slot_map[0] >= 0, slot_map[0] ^ (s * tiles), -1)
    return row[:, None], target[None, :]


def on_device(stiffness_tiles, damping_tiles, tile_map, inv_mass, spectral_shift, basis, compact):
    rows_count = lax.axis_size("rows")
    sub_count = lax.axis_size("sub")
    devices = rows_count * sub_count
    half = sub_count // 2
    tile_size = stiffness_tiles.shape[-1]
    slots = stiffness_tiles.shape[2]
    held_count, local_rows = basis.shape
    tiles = local_rows // tile_size
    unknowns = local_rows * devices
    height = -(-held_count // (2 * SUBL)) * 2 * SUBL
    block = 2 * SUBL
    every = ("rows", "sub")

    def swap(value, partner):
        pairs = []
        for r in range(rows_count):
            for s in range(sub_count):
                to_r, to_s = partner(r, s)
                pairs.append((r * sub_count + s, to_r * sub_count + to_s))
        return lax.ppermute(value, every, pairs)

    def beside(r, s):
        return r ^ 1 if s % 2 == 0 else (((r + 1) ^ 1) - 1) % rows_count

    damping = damping_tiles[0, 0]
    stiffness = stiffness_tiles[0, 0]
    shift = spectral_shift.reshape(1)
    mass = inv_mass.reshape(tiles, tile_size)
    quarter = lax.axis_index("sub").reshape(1)
    source, target = window_rows(tile_map[0, 0], rows_count, sub_count, tiles)
    field = ((tiles, tile_size), F32)
    vector = ((2 * tiles, tile_size), BF16)
    square = ((height, LANES), F32)

    columns = compact.transpose(2, 0, 1)
    upper_vec, vectors, basis = call(
        start_kernel,
        [field, vector, (basis.shape, F32)],
        (columns, basis),
        [VM((2, held_count), F32), pltpu.SemaphoreType.DMA((tiles // SUBL + 1,))],
        far=(0, 1),
    )
    padding = ((0, 0), (0, height - compact.shape[1]), (0, LANES - compact.shape[2]))
    halves = jnp.pad(compact, padding)
    upper_half, lower_half = halves[0], halves[1]
    gram = jnp.dot(basis, basis.T, precision=lax.Precision.HIGHEST)
    column = weights = added = None
    for iteration in range(ITERS):
        packed = iteration == 0
        last = iteration == ITERS - 1
        pair = jnp.stack([vectors, swap(vectors, lambda r, s: (r, s ^ 1))])
        mine = [
            swap(vectors, lambda r, s, k=k: (r, s ^ (2 * k)))[None] for k in range(1, half)
        ] + [swap(pair, lambda r, s, k=k: (beside(r, s), s ^ (2 * k))) for k in range(half)]
        mine = jnp.concatenate(mine, axis=0)
        other = swap(mine, lambda r, s: (r, s ^ 1))
        depth = tiles + SUBL if packed else tiles
        scratch = [
            VM((slots, 2 * LANES), BF16),
            VM((slots, LANES), F32),
            VM((2, slots, tile_size, tile_size), BF16),
            pltpu.SemaphoreType.DMA((2, slots // block)),
        ]
        args = [source, target, quarter, pair, mine, other, damping, stiffness]
        if packed:
            args.append(gram)
            scratch.append(VM((height, LANES), F32))
        parts = call(
            functools.partial(tile_kernel, block, sub_count, packed),
            [((depth, LANES), F32)] * sub_count,
            args,
            scratch,
            far=(6, 7),
        )
        parts = [parts[0]] + [
            swap(parts[k], lambda r, s, k=k: (r, s ^ k)) for k in range(1, sub_count)
        ]
        packet = (devices, SUBL, LANES) if packed else (devices, 1, LANES)
        args = [shift, *parts, upper_vec, mass, basis]
        if not packed:
            args.append(column)
        image, sent = call(
            functools.partial(inner_kernel, sub_count, packed), [field, (packet, F32)], args
        )
        received = lax.all_to_all(sent, every, 0, 0)
        args = [shift, received, image, basis, upper_half, lower_half]
        if not packed:
            args += [gram, column, weights, columns, added]
        total = held_count + ITERS
        if last:
            outs = [
                ((ITERS, local_rows), F32),
                ((total - 1, 2, total), F32),
                ((ITERS, total - 1), F32),
            ]
        else:
            outs = [field, field, vector, square, square, square]
            outs += [((SUBL, LANES), F32), ((1, 2, LANES), F32)]
        outs = call(
            functools.partial(update_kernel, unknowns, sub_count, iteration, last),
            outs,
            args,
            final=last,
        )
        if not last:
            column, upper_vec, vectors, upper_half, lower_half, gram, weights, added = outs
    new_basis, compact_out, hessenberg = outs
    return new_basis, compact_out.transpose(1, 2, 0), hessenberg.T


def solution(mesh):
    in_specs = (
        P("rows", "sub", None, None, None),
        P("rows", "sub", None, None, None),
        P("rows", "sub", None, None),
        P(("rows", "sub")),
        P(),
        P(None, ("rows", "sub")),
        P(),
    )
    out_specs = (P(None, ("rows", "sub")), P(), P())
    return jax.shard_map(
        on_device, mesh=mesh, in_specs=in_specs, out_specs=out_specs, check_vma=False
    )
```

```python
import functools

import jax
import jax.numpy as jnp
from jax import lax
from jax.experimental import pallas as pl
from jax.experimental.pallas import tpu as pltpu
from jax.sharding import PartitionSpec as P

ITERS = 2
LANES = 128
SUBL = 8
F32 = jnp.float32
BF16 = jnp.bfloat16
VM = pltpu.VMEM
SM = pltpu.SMEM
GRANT = 16 * 1024 * 1024
JOIN_GRANT = 1024 * 1024


def iota(shape, axis):
    return lax.broadcasted_iota(jnp.int32, shape, axis)


def lane_sum(x):
    return jnp.sum(x, axis=1, keepdims=True)


def sub_sum(x):
    return jnp.sum(x, axis=0, keepdims=True)


def row_to_col(row, height):
    shape = (height, LANES)
    return lane_sum(jnp.where(iota(shape, 0) == iota(shape, 1), row, 0.0))


def col_to_row(col, height):
    shape = (height, LANES)
    return sub_sum(jnp.where(iota(shape, 0) == iota(shape, 1), col, 0.0))


def at_sublane(col, index):
    return jnp.sum(jnp.where(iota(col.shape, 0) == index, col, 0.0), axis=0, keepdims=True)


def gather_rows(parts):
    shift = 1
    while len(parts) > 1:
        low = (iota((SUBL, LANES), 0) // shift) % 2 == 0
        merged = []
        for a, b in zip(parts[0::2], parts[1::2]):
            moved = pltpu.roll(jnp.where(low, b, a), SUBL - shift, axis=0)
            merged.append(jnp.where(low, a, b) + moved)
        parts = merged
        shift *= 2
    return parts[0]


def block_rows(held_ref):
    n = held_ref.shape[0]
    return [(i, min(SUBL, n - i)) for i in range(0, n, SUBL)]


def combine(held_ref, cols, group):
    out = []
    totals = [[] for _ in cols]
    for k in range(SUBL):
        lanes = pl.ds((group * SUBL + k) * LANES, LANES)
        sums = [None] * len(cols)
        for start, size in block_rows(held_ref):
            block = held_ref[pl.ds(start, size), lanes]
            if size < SUBL:
                block = jnp.concatenate(
                    [block, jnp.zeros((SUBL - size, LANES), F32)], axis=0
                )
            for i, col in enumerate(cols):
                term = block * col[start : start + SUBL]
                sums[i] = term if sums[i] is None else sums[i] + term
        for i in range(len(cols)):
            totals[i].append(sums[i])
    for i in range(len(cols)):
        out.append(gather_rows(totals[i]))
    return out


def start_kernel(compact_ref, basis_ref, upper_ref, vec_ref, held_ref, last_ref, sems):
    tiles = upper_ref.shape[0]
    n = held_ref.shape[0]
    groups = tiles // SUBL
    height = -(-n // SUBL) * SUBL
    span = SUBL * LANES
    first = pltpu.make_async_copy(
        compact_ref.at[compact_ref.shape[0] - 1], last_ref, sems.at[groups]
    )
    first.start()
    copies = []
    for group in range(groups):
        lanes = pl.ds(group * span, span)
        copies.append(
            pltpu.make_async_copy(basis_ref.at[:, lanes], held_ref.at[:, lanes], sems.at[group])
        )
        copies[-1].start()
    first.wait()
    rows = jnp.pad(last_ref[...], ((0, 0), (0, LANES - n)))
    cols = [
        jnp.broadcast_to(row_to_col(rows[i : i + 1], height), (height, LANES)) for i in range(2)
    ]
    for group in range(groups):
        copies[group].wait()
        upper, lower = combine(held_ref, cols, group)
        at = group * SUBL
        upper_ref[at : at + SUBL] = upper
        vec_ref[at : at + SUBL] = upper.astype(BF16)
        vec_ref[tiles + at : tiles + at + SUBL] = lower.astype(BF16)


def join_kernel(*refs):
    out_ref = refs[-1]
    at = 0
    for ref in refs[:-2]:
        out_ref[at : at + ref.shape[0]] = ref[...]
        at += ref.shape[0]


def load_kernel(pieces, source_ref, *refs):
    target_ref, sems = refs[-2:]
    size = target_ref.shape[0] // pieces
    copies = []
    for i in range(pieces):
        at = pl.ds(i * size, size)
        copies.append(pltpu.make_async_copy(source_ref.at[at], target_ref.at[at], sems.at[i]))
        copies[-1].start()
    for copy in copies:
        copy.wait()


def tile_kernel(
    block,
    sub_count,
    packed,
    source_ref,
    target_ref,
    quarter_ref,
    pair_ref,
    mine_ref,
    other_ref,
    damping_ref,
    front_ref,
    stiffness_ref,
    *rest,
):
    if packed:
        gram_ref, rest = rest[0], rest[1:]
    outs, rest = rest[:sub_count], rest[sub_count:]
    picked_ref, product_ref, buffer_ref, sems = rest[:4]
    tiles = pair_ref.shape[1] // 2
    slots = damping_ref.shape[0]
    part_tiles = sub_count * tiles

    half = slots // 2
    copies = []
    for i in range(half // block):
        at = pl.ds(i * block, block)
        copies.append(
            pltpu.make_async_copy(
                damping_ref.at[pl.ds(half + i * block, block)], buffer_ref.at[at], sems.at[i]
            )
        )
        copies[-1].start()

    window = []
    for ref in (pair_ref, mine_ref, other_ref):
        for i in range(ref.shape[0]):
            window.append(jnp.concatenate([ref[i, :tiles], ref[i, tiles:]], axis=1))
    window = jnp.concatenate(window, axis=0)
    depth = window.shape[0]
    chooser = jnp.where(iota((slots, depth), 1) == source_ref[...], 1.0, 0.0).astype(BF16)
    picked_ref[...] = jnp.dot(chooser, window, preferred_element_type=F32).astype(BF16)

    dims = (((1,), (1,)), ((), ()))
    for step in range(slots // block):
        at = pl.ds(step * block, block)
        if step * block == half:
            for copy in copies:
                copy.wait()
        ref = buffer_ref if step * block >= half else front_ref
        left = ref[pl.ds(step * block % half, block)]
        both = jnp.concatenate(
            [value.reshape(block * LANES, LANES) for value in (left, stiffness_ref[at])], axis=1
        )
        result = lax.dot_general(picked_ref[at], both, dims, preferred_element_type=F32)
        own = jnp.zeros((block, LANES), F32)
        for t in range(block):
            own = jnp.where(
                iota((block, LANES), 0) == t, result[:, t * LANES : (t + 1) * LANES], own
            )
        product_ref[at] = own

    selector = jnp.where(iota((part_tiles, slots), 0) == target_ref[...], 1.0, 0.0).astype(BF16)
    left = product_ref[...]
    summed = jnp.zeros((part_tiles, LANES), F32)
    for _ in range(3):
        piece = left.astype(BF16)
        summed = summed + jnp.dot(selector, piece, preferred_element_type=F32)
        left = left - piece.astype(F32)
    for k in range(sub_count):
        outs[k][:tiles] = summed[k * tiles : (k + 1) * tiles]
    if packed:
        square_ref = rest[4]
        n = gram_ref.shape[0]
        square_ref[...] = jnp.zeros(square_ref.shape, F32)
        square_ref[:n, :n] = gram_ref[...]
        share = square_ref.shape[0] // sub_count
        for k in range(sub_count):
            start = pl.multiple_of((quarter_ref[0] ^ k) * share, SUBL)
            low = square_ref[pl.ds(start, SUBL)]
            high = square_ref[pl.ds(start + SUBL, SUBL)]
            outs[k][tiles:] = low + pltpu.roll(high, LANES // 2, axis=1)


def inner_kernel(sub_count, packed, shift_ref, *refs):
    parts = refs[:sub_count]
    upper_ref, mass_ref, held_ref = refs[sub_count : sub_count + 3]
    refs = refs[sub_count + 3 :]
    if not packed:
        column_ref, refs = refs[0], refs[1:]
    image_ref, packet_ref = refs
    tiles = upper_ref.shape[0]
    n = held_ref.shape[0]
    total = parts[0][:tiles]
    for k in range(1, sub_count):
        total = total + parts[k][:tiles]
    image = shift_ref[0] * upper_ref[...] - mass_ref[...] * total
    image_ref[...] = image
    square = lane_sum(sub_sum(image * image))
    blocks = block_rows(held_ref)
    sums = [None] * len(blocks)
    for k in range(tiles):
        row = image_ref[k : k + 1]
        for i, (start, size) in enumerate(blocks):
            term = held_ref[pl.ds(start, size), pl.ds(k * LANES, LANES)] * row
            sums[i] = term if sums[i] is None else sums[i] + term
    cols = []
    for total_block, (start, size) in zip(sums, blocks):
        col = lane_sum(total_block)
        if size < SUBL:
            col = jnp.concatenate([col, jnp.zeros((SUBL - size, 1), F32)], axis=0)
        cols.append(col)
    lane = iota((SUBL, LANES), 1)
    if packed:
        packet = parts[0][tiles:]
        for k in range(1, sub_count):
            packet = packet + parts[k][tiles:]
        for i, col in enumerate(cols):
            spot = (i % 2) * (LANES // 2) + n + i // 2
            packet = jnp.where(lane == spot, col, packet)
        spot = n + (len(cols) + 1) // 2
        first = iota((SUBL, LANES), 0) == 0
        packet = jnp.where(jnp.logical_and(lane == spot, first), square, packet)
        packet_ref[...] = jnp.broadcast_to(packet[None], packet_ref.shape)
    else:
        height = SUBL * len(cols)
        row = col_to_row(jnp.concatenate(cols, axis=0), height)
        extra = lane_sum(sub_sum(image * column_ref[...]))
        row = jnp.where(lane[:1] == n, extra, row)
        row = jnp.where(lane[:1] == LANES - 1, square, row)
        packet_ref[...] = jnp.broadcast_to(row[None], packet_ref.shape)


def update_kernel(unknowns, sub_count, iteration, last, shift_ref, *refs):
    packet_ref, image_ref, held_ref, upper_half_ref, lower_half_ref = refs[:5]
    refs = refs[5:]
    n0 = held_ref.shape[0]
    n = n0 + iteration
    tiles = image_ref.shape[0]
    height = -(-n0 // (2 * SUBL)) * 2 * SUBL
    shape = (height, LANES)
    lane = iota(shape, 1)
    subl = iota(shape, 0)
    inverse = 1.0 / unknowns
    if iteration == 0:
        out_refs = refs
        count = packet_ref.shape[0] // sub_count
        blocks = []
        for s in range(sub_count):
            total = packet_ref[s]
            for r in range(1, count):
                total = total + packet_ref[r * sub_count + s]
            blocks.append(total)
        every = blocks[0]
        for s in range(1, sub_count):
            every = every + blocks[s]
        lane8 = iota((SUBL, LANES), 1)
        gram = []
        for total in blocks:
            gram.append(jnp.where(lane8 < n, total, 0.0))
            gram.append(jnp.where(lane8 < n, pltpu.roll(total, LANES // 2, axis=1), 0.0))
        gram = jnp.concatenate(gram, axis=0) * inverse
        pieces = -(-n0 // SUBL)
        cols = []
        for i in range(height // SUBL):
            spot = (i % 2) * (LANES // 2) + n + i // 2
            cols.append(lane_sum(jnp.where(lane8 == spot, every, 0.0)))
        first_col = jnp.concatenate(cols, axis=0) * inverse
        first_row = col_to_row(first_col, height)
        spot = n + (pieces + 1) // 2
        self_mean = sub_sum(lane_sum(jnp.where(lane8 == spot, every, 0.0))) * inverse
    else:
        gram_ref, column_ref, weights_ref = refs[:3]
        out_refs = refs[5:]
        total = packet_ref[0]
        for i in range(1, packet_ref.shape[0]):
            total = total + packet_ref[i]
        gram = gram_ref[...]
        first_row = jnp.where(lane[:1] < n, total, 0.0) * inverse
        first_col = row_to_col(first_row, height)
        self_mean = lane_sum(jnp.where(lane[:1] == LANES - 1, total, 0.0)) * inverse
    coef_col = first_col + (first_col - lane_sum(gram * first_row))
    coef_row = first_row + (first_row - sub_sum(gram * first_col))
    gram_coef = lane_sum(gram * coef_row)
    mean_square = self_mean - 2.0 * sub_sum(coef_col * first_col) + sub_sum(coef_col * gram_coef)
    norm = jnp.sqrt(mean_square + 1e-06)
    upper_half = upper_half_ref[...]
    lower_half = lower_half_ref[...]
    columns = n - 1
    shift = shift_ref[0]
    tail = lane_sum(jnp.where(lane == columns - 1, upper_half + shift * lower_half, 0.0))
    upper_coef = jnp.where(subl[:, :1] == n, norm, coef_col)
    lower_coef = tail
    weights = jnp.zeros((1, LANES), F32)
    for _ in range(2):
        projection = sub_sum(upper_half * upper_coef + lower_half * lower_coef)
        upper_coef = upper_coef - lane_sum(upper_half * projection)
        lower_coef = lower_coef - lane_sum(lower_half * projection)
        weights = weights + projection
    beta = jnp.sqrt(sub_sum(upper_coef * upper_coef + lower_coef * lower_coef) + 1e-06)
    upper_new = upper_coef / beta
    lower_new = lower_coef / beta
    upper_half = jnp.where(lane == columns, upper_new, upper_half)
    lower_half = jnp.where(lane == columns, lower_new, lower_half)
    weights = jnp.where(lane[:1] == columns, beta, weights)
    coef_wide = jnp.broadcast_to(coef_col, shape)
    if not last:
        column_ref, upper_ref, vec_ref = out_refs[:3]
        upper_half_out, lower_half_out, gram_out, weights_out, added_ref = out_refs[3:]
        added_ref[0, 0:1] = col_to_row(upper_new, height)
        added_ref[0, 1:2] = col_to_row(lower_new, height)
        upper_half_out[...] = upper_half
        lower_half_out[...] = lower_half
        weights_out[...] = jnp.broadcast_to(weights, (SUBL, LANES))
        cross_col = (first_col - gram_coef) / norm
        cross_row = (first_row - sub_sum(gram * coef_col)) / norm
        gram = jnp.where(lane == n, cross_col, gram)
        gram = jnp.where(subl == n, cross_row, gram)
        corner = jnp.logical_and(lane == n, subl == n)
        gram_out[...] = jnp.where(corner, mean_square / (norm * norm), gram)
        upper_wide = jnp.broadcast_to(upper_new, shape)
        lower_wide = jnp.broadcast_to(lower_new, shape)
        upper_last = at_sublane(upper_new, n)
        lower_last = at_sublane(lower_new, n)
        for group in range(tiles // SUBL):
            at = group * SUBL
            along, upper, lower = combine(held_ref, [coef_wide, upper_wide, lower_wide], group)
            column = (image_ref[at : at + SUBL] - along) / norm
            upper = upper + column * upper_last
            lower = lower + column * lower_last
            column_ref[at : at + SUBL] = column
            upper_ref[at : at + SUBL] = upper
            vec_ref[at : at + SUBL] = upper.astype(BF16)
            vec_ref[tiles + at : tiles + at + SUBL] = lower.astype(BF16)
    else:
        basis_ref, compact_ref, hess_ref = out_refs
        before_ref, first_ref = refs[3:5]
        out_refs = None
        old, pair, width = before_ref.shape
        compact_ref[:old, :, :width] = before_ref[...]
        compact_ref[:old, :, width:] = jnp.zeros((old, pair, n + 1 - width), F32)
        compact_ref[old : old + 1] = first_ref[:, :, : n + 1]
        compact_ref[old + 1, 0:1] = col_to_row(upper_new, height)[:, : n + 1]
        compact_ref[old + 1, 1:2] = col_to_row(lower_new, height)[:, : n + 1]
        hess_ref[0:1] = weights_ref[:1, :n]
        hess_ref[1:2] = weights[:, :n]
        coef_last = at_sublane(coef_col, n0)
        for group in range(tiles // SUBL):
            at = group * SUBL
            (along,) = combine(held_ref, [coef_wide], group)
            before = column_ref[at : at + SUBL]
            column = (image_ref[at : at + SUBL] - along - before * coef_last) / norm
            for k in range(SUBL):
                lanes = pl.ds((at + k) * LANES, LANES)
                basis_ref[0:1, lanes] = before[k : k + 1]
                basis_ref[1:2, lanes] = column[k : k + 1]


def call(body, outs, args, scratch=(), final=False, far=(), grant=GRANT, cost=None):
    specs, values = [], []
    for i, value in enumerate(args):
        space = pltpu.HBM if i in far else SM if value.shape == (1,) else VM
        specs.append(pl.BlockSpec(memory_space=space))
        values.append(
            value if space == SM else pltpu.with_memory_space_constraint(value, space)
        )
    return pl.pallas_call(
        body,
        out_shape=[
            jax.ShapeDtypeStruct(shape, dtype) if final else VM(shape, dtype)
            for shape, dtype in outs
        ],
        in_specs=specs,
        out_specs=[pl.BlockSpec(memory_space=VM)] * len(outs),
        scratch_shapes=list(scratch),
        compiler_params=pltpu.CompilerParams(vmem_limit_bytes=grant),
        cost_estimate=cost,
    )(*values)


def load(array, count, pieces, before):
    shape = (count,) + array.shape[1:]
    return call(
        functools.partial(load_kernel, pieces),
        [(shape, array.dtype)],
        [array] + before,
        [pltpu.SemaphoreType.DMA((pieces,))],
        far=(0,),
        grant=JOIN_GRANT,
        cost=pl.CostEstimate(
            flops=0,
            bytes_accessed=4 * array.size * count // array.shape[0],
            transcendentals=0,
        ),
    )[0]


def join(values, after):
    shape = (sum(value.shape[0] for value in values),) + values[0].shape[1:]
    return call(join_kernel, [(shape, values[0].dtype)], values + [after], grant=JOIN_GRANT)[0]


def window_rows(slot_map, rows_count, sub_count, tiles):
    r = lax.axis_index("rows")
    s = lax.axis_index("sub")
    half = sub_count // 2
    mine = 2
    other = mine + half - 1 + sub_count
    source = slot_map[1]
    part = source // (sub_count * tiles) - 1
    sub = (source // tiles) % sub_count
    beside = (sub ^ s) & 1
    same = sub ^ s
    within = jnp.where(
        same < 2, same, jnp.where(beside == 0, mine, other) + (same >> 1) - 1
    )
    towards = jnp.where((r + s) % 2 == 0, 1, -1)
    away = half - 1 + jnp.where(part == towards, mine + same, other + (same ^ 1))
    slice_at = jnp.where(part == 0, within, away)
    inside = (r + part >= 0) & (r + part < rows_count)
    row = jnp.where(inside, slice_at * tiles + source % tiles, -1)
    target = jnp.where(slot_map[0] >= 0, slot_map[0] ^ (s * tiles), -1)
    return row[:, None], target[None, :]


def on_device(stiffness_tiles, damping_tiles, tile_map, inv_mass, spectral_shift, basis, compact):
    rows_count = lax.axis_size("rows")
    sub_count = lax.axis_size("sub")
    devices = rows_count * sub_count
    half = sub_count // 2
    tile_size = stiffness_tiles.shape[-1]
    slots = stiffness_tiles.shape[2]
    held_count, local_rows = basis.shape
    tiles = local_rows // tile_size
    unknowns = local_rows * devices
    height = -(-held_count // (2 * SUBL)) * 2 * SUBL
    block = 2 * SUBL
    every = ("rows", "sub")

    def swap(value, partner):
        pairs = []
        for r in range(rows_count):
            for s in range(sub_count):
                to_r, to_s = partner(r, s)
                pairs.append((r * sub_count + s, to_r * sub_count + to_s))
        return lax.ppermute(value, every, pairs)

    def beside(r, s):
        return r ^ 1 if s % 2 == 0 else (((r + 1) ^ 1) - 1) % rows_count

    damping = damping_tiles[0, 0]
    stiffness = stiffness_tiles[0, 0]
    shift = spectral_shift.reshape(1)
    mass = inv_mass.reshape(tiles, tile_size)
    quarter = lax.axis_index("sub").reshape(1)
    source, target = window_rows(tile_map[0, 0], rows_count, sub_count, tiles)
    field = ((tiles, tile_size), F32)
    vector = ((2 * tiles, tile_size), BF16)
    square = ((height, LANES), F32)

    columns = compact.transpose(2, 0, 1)
    upper_vec, vectors, basis = call(
        start_kernel,
        [field, vector, (basis.shape, F32)],
        (columns, basis),
        [VM((2, held_count), F32), pltpu.SemaphoreType.DMA((tiles // SUBL + 1,))],
        far=(0, 1),
    )
    padding = ((0, 0), (0, height - compact.shape[1]), (0, LANES - compact.shape[2]))
    halves = jnp.pad(compact, padding)
    upper_half, lower_half = halves[0], halves[1]
    pieces = slots // block
    column = weights = added = None
    for iteration in range(ITERS):
        packed = iteration == 0
        last = iteration == ITERS - 1
        pair = jnp.stack([vectors, swap(vectors, lambda r, s: (r, s ^ 1))])
        mine = [
            swap(vectors[None], lambda r, s, k=k: (r, s ^ (2 * k))) for k in range(1, half)
        ] + [swap(pair, lambda r, s, k=k: (beside(r, s), s ^ (2 * k))) for k in range(half)]
        before = [pair]
        if packed:
            _, late = lax.optimization_barrier((pair, basis))
            gram = jnp.dot(late, late.T, precision=lax.Precision.HIGHEST)
            before += [gram, source, target, upper_half, lower_half]
        loaded = load(stiffness, slots, pieces, before)
        mine = join(mine, loaded)
        other = swap(mine, lambda r, s: (r, s ^ 1))
        loaded_half = load(damping, slots // 2, pieces // 2, [mine])
        depth = tiles + SUBL if packed else tiles
        scratch = [
            VM((slots, 2 * LANES), BF16),
            VM((slots, LANES), F32),
            VM((slots // 2, tile_size, tile_size), BF16),
            pltpu.SemaphoreType.DMA((pieces // 2,)),
        ]
        args = [source, target, quarter, pair, mine, other, damping, loaded_half, loaded]
        if packed:
            args.append(gram)
            scratch.append(VM((height, LANES), F32))
        parts = call(
            functools.partial(tile_kernel, block, sub_count, packed),
            [((depth, LANES), F32)] * sub_count,
            args,
            scratch,
            far=(6,),
        )
        parts = [parts[0]] + [
            swap(parts[k], lambda r, s, k=k: (r, s ^ k)) for k in range(1, sub_count)
        ]
        packet = (devices, SUBL, LANES) if packed else (devices, 1, LANES)
        args = [shift, *parts, upper_vec, mass, basis]
        if not packed:
            args.append(column)
        image, sent = call(
            functools.partial(inner_kernel, sub_count, packed), [field, (packet, F32)], args
        )
        received = lax.all_to_all(sent, every, 0, 0)
        args = [shift, received, image, basis, upper_half, lower_half]
        if not packed:
            args += [gram, column, weights, columns, added]
        total = held_count + ITERS
        if last:
            outs = [
                ((ITERS, local_rows), F32),
                ((total - 1, 2, total), F32),
                ((ITERS, total - 1), F32),
            ]
        else:
            outs = [field, field, vector, square, square, square]
            outs += [((SUBL, LANES), F32), ((1, 2, LANES), F32)]
        outs = call(
            functools.partial(update_kernel, unknowns, sub_count, iteration, last),
            outs,
            args,
            final=last,
        )
        if not last:
            column, upper_vec, vectors, upper_half, lower_half, gram, weights, added = outs
    new_basis, compact_out, hessenberg = outs
    return new_basis, compact_out.transpose(1, 2, 0), hessenberg.T


def solution(mesh):
    in_specs = (
        P("rows", "sub", None, None, None),
        P("rows", "sub", None, None, None),
        P("rows", "sub", None, None),
        P(("rows", "sub")),
        P(),
        P(None, ("rows", "sub")),
        P(),
    )
    out_specs = (P(None, ("rows", "sub")), P(), P())
    return jax.shard_map(
        on_device, mesh=mesh, in_specs=in_specs, out_specs=out_specs, check_vma=False
    )
```

```python
import functools

import jax
import jax.numpy as jnp
from jax import lax
from jax.experimental import pallas as pl
from jax.experimental.pallas import tpu as pltpu
from jax.sharding import PartitionSpec as P

ITERS = 2
LANES = 128
SUBL = 8
F32 = jnp.float32
BF16 = jnp.bfloat16
VM = pltpu.VMEM
SM = pltpu.SMEM
GRANT = 16 * 1024 * 1024
JOIN_GRANT = 1024 * 1024


def iota(shape, axis):
    return lax.broadcasted_iota(jnp.int32, shape, axis)


def lane_sum(x):
    return jnp.sum(x, axis=1, keepdims=True)


def sub_sum(x):
    return jnp.sum(x, axis=0, keepdims=True)


def row_to_col(row, height):
    shape = (height, LANES)
    return lane_sum(jnp.where(iota(shape, 0) == iota(shape, 1), row, 0.0))


def col_to_row(col, height):
    shape = (height, LANES)
    return sub_sum(jnp.where(iota(shape, 0) == iota(shape, 1), col, 0.0))


def at_sublane(col, index):
    return jnp.sum(jnp.where(iota(col.shape, 0) == index, col, 0.0), axis=0, keepdims=True)


def gather_rows(parts):
    shift = 1
    while len(parts) > 1:
        low = (iota((SUBL, LANES), 0) // shift) % 2 == 0
        merged = []
        for a, b in zip(parts[0::2], parts[1::2]):
            moved = pltpu.roll(jnp.where(low, b, a), SUBL - shift, axis=0)
            merged.append(jnp.where(low, a, b) + moved)
        parts = merged
        shift *= 2
    return parts[0]


def block_rows(held_ref):
    n = held_ref.shape[0]
    return [(i, min(SUBL, n - i)) for i in range(0, n, SUBL)]


def combine(held_ref, cols, group):
    out = []
    totals = [[] for _ in cols]
    for k in range(SUBL):
        lanes = pl.ds((group * SUBL + k) * LANES, LANES)
        sums = [None] * len(cols)
        for start, size in block_rows(held_ref):
            block = held_ref[pl.ds(start, size), lanes]
            if size < SUBL:
                block = jnp.concatenate(
                    [block, jnp.zeros((SUBL - size, LANES), F32)], axis=0
                )
            for i, col in enumerate(cols):
                term = block * col[start : start + SUBL]
                sums[i] = term if sums[i] is None else sums[i] + term
        for i in range(len(cols)):
            totals[i].append(sums[i])
    for i in range(len(cols)):
        out.append(gather_rows(totals[i]))
    return out


def start_kernel(compact_ref, basis_ref, upper_ref, vec_ref, held_ref, last_ref, sems):
    tiles = upper_ref.shape[0]
    n = held_ref.shape[0]
    groups = tiles // SUBL
    height = -(-n // SUBL) * SUBL
    span = SUBL * LANES
    first = pltpu.make_async_copy(
        compact_ref.at[compact_ref.shape[0] - 1], last_ref, sems.at[groups]
    )
    first.start()
    copies = []
    for group in range(groups):
        lanes = pl.ds(group * span, span)
        copies.append(
            pltpu.make_async_copy(basis_ref.at[:, lanes], held_ref.at[:, lanes], sems.at[group])
        )
        copies[-1].start()
    first.wait()
    rows = jnp.pad(last_ref[...], ((0, 0), (0, LANES - n)))
    cols = [
        jnp.broadcast_to(row_to_col(rows[i : i + 1], height), (height, LANES)) for i in range(2)
    ]
    for group in range(groups):
        copies[group].wait()
        upper, lower = combine(held_ref, cols, group)
        at = group * SUBL
        upper_ref[at : at + SUBL] = upper
        vec_ref[at : at + SUBL] = upper.astype(BF16)
        vec_ref[tiles + at : tiles + at + SUBL] = lower.astype(BF16)


def join_kernel(*refs):
    out_ref = refs[-1]
    at = 0
    for ref in refs[:-2]:
        out_ref[at : at + ref.shape[0]] = ref[...]
        at += ref.shape[0]


def load_kernel(pieces, source_ref, *refs):
    target_ref, sems = refs[-2:]
    size = target_ref.shape[0] // pieces
    copies = []
    for i in range(pieces):
        at = pl.ds(i * size, size)
        copies.append(pltpu.make_async_copy(source_ref.at[at], target_ref.at[at], sems.at[i]))
        copies[-1].start()
    for copy in copies:
        copy.wait()


def tile_kernel(
    block,
    sub_count,
    packed,
    source_ref,
    target_ref,
    quarter_ref,
    pair_ref,
    mine_ref,
    other_ref,
    damping_ref,
    front_ref,
    stiffness_ref,
    *rest,
):
    if packed:
        gram_ref, rest = rest[0], rest[1:]
    outs, rest = rest[:sub_count], rest[sub_count:]
    picked_ref, product_ref, buffer_ref, sems = rest[:4]
    tiles = pair_ref.shape[1] // 2
    slots = damping_ref.shape[0]
    part_tiles = sub_count * tiles

    half = slots // 2
    copies = []
    for i in range(half // block):
        at = pl.ds(i * block, block)
        copies.append(
            pltpu.make_async_copy(
                damping_ref.at[pl.ds(half + i * block, block)], buffer_ref.at[at], sems.at[i]
            )
        )
        copies[-1].start()

    window = []
    for ref in (pair_ref, mine_ref, other_ref):
        for i in range(ref.shape[0]):
            window.append(jnp.concatenate([ref[i, :tiles], ref[i, tiles:]], axis=1))
    window = jnp.concatenate(window, axis=0)
    depth = window.shape[0]
    chooser = jnp.where(iota((slots, depth), 1) == source_ref[...], 1.0, 0.0).astype(BF16)
    picked_ref[...] = jnp.dot(chooser, window, preferred_element_type=F32).astype(BF16)

    dims = (((1,), (1,)), ((), ()))
    for step in range(slots // block):
        at = pl.ds(step * block, block)
        if step * block == half:
            for copy in copies:
                copy.wait()
        ref = buffer_ref if step * block >= half else front_ref
        left = ref[pl.ds(step * block % half, block)]
        both = jnp.concatenate(
            [value.reshape(block * LANES, LANES) for value in (left, stiffness_ref[at])], axis=1
        )
        result = lax.dot_general(picked_ref[at], both, dims, preferred_element_type=F32)
        own = jnp.zeros((block, LANES), F32)
        for t in range(block):
            own = jnp.where(
                iota((block, LANES), 0) == t, result[:, t * LANES : (t + 1) * LANES], own
            )
        product_ref[at] = own

    selector = jnp.where(iota((part_tiles, slots), 0) == target_ref[...], 1.0, 0.0).astype(BF16)
    left = product_ref[...]
    summed = jnp.zeros((part_tiles, LANES), F32)
    for _ in range(3):
        piece = left.astype(BF16)
        summed = summed + jnp.dot(selector, piece, preferred_element_type=F32)
        left = left - piece.astype(F32)
    for k in range(sub_count):
        outs[k][:tiles] = summed[k * tiles : (k + 1) * tiles]
    if packed:
        square_ref = rest[4]
        n = gram_ref.shape[0]
        square_ref[...] = jnp.zeros(square_ref.shape, F32)
        square_ref[:n, :n] = gram_ref[...]
        share = square_ref.shape[0] // sub_count
        for k in range(sub_count):
            start = pl.multiple_of((quarter_ref[0] ^ k) * share, SUBL)
            low = square_ref[pl.ds(start, SUBL)]
            high = square_ref[pl.ds(start + SUBL, SUBL)]
            outs[k][tiles:] = low + pltpu.roll(high, LANES // 2, axis=1)


def inner_kernel(sub_count, packed, shift_ref, *refs):
    parts = refs[:sub_count]
    upper_ref, mass_ref, held_ref = refs[sub_count : sub_count + 3]
    refs = refs[sub_count + 3 :]
    if not packed:
        column_ref, refs = refs[0], refs[1:]
    image_ref, packet_ref = refs
    tiles = upper_ref.shape[0]
    n = held_ref.shape[0]
    total = parts[0][:tiles]
    for k in range(1, sub_count):
        total = total + parts[k][:tiles]
    image = shift_ref[0] * upper_ref[...] - mass_ref[...] * total
    image_ref[...] = image
    square = lane_sum(sub_sum(image * image))
    blocks = block_rows(held_ref)
    sums = [None] * len(blocks)
    for k in range(tiles):
        row = image_ref[k : k + 1]
        for i, (start, size) in enumerate(blocks):
            term = held_ref[pl.ds(start, size), pl.ds(k * LANES, LANES)] * row
            sums[i] = term if sums[i] is None else sums[i] + term
    cols = []
    for total_block, (start, size) in zip(sums, blocks):
        col = lane_sum(total_block)
        if size < SUBL:
            col = jnp.concatenate([col, jnp.zeros((SUBL - size, 1), F32)], axis=0)
        cols.append(col)
    lane = iota((SUBL, LANES), 1)
    if packed:
        packet = parts[0][tiles:]
        for k in range(1, sub_count):
            packet = packet + parts[k][tiles:]
        for i, col in enumerate(cols):
            spot = (i % 2) * (LANES // 2) + n + i // 2
            packet = jnp.where(lane == spot, col, packet)
        spot = n + (len(cols) + 1) // 2
        first = iota((SUBL, LANES), 0) == 0
        packet = jnp.where(jnp.logical_and(lane == spot, first), square, packet)
        packet_ref[...] = jnp.broadcast_to(packet[None], packet_ref.shape)
    else:
        height = SUBL * len(cols)
        row = col_to_row(jnp.concatenate(cols, axis=0), height)
        extra = lane_sum(sub_sum(image * column_ref[...]))
        row = jnp.where(lane[:1] == n, extra, row)
        row = jnp.where(lane[:1] == LANES - 1, square, row)
        packet_ref[...] = jnp.broadcast_to(row[None], packet_ref.shape)


def update_kernel(unknowns, sub_count, iteration, last, shift_ref, *refs):
    packet_ref, image_ref, held_ref, upper_half_ref, lower_half_ref = refs[:5]
    refs = refs[5:]
    n0 = held_ref.shape[0]
    n = n0 + iteration
    tiles = image_ref.shape[0]
    height = -(-n0 // (2 * SUBL)) * 2 * SUBL
    shape = (height, LANES)
    lane = iota(shape, 1)
    subl = iota(shape, 0)
    inverse = 1.0 / unknowns
    if iteration == 0:
        out_refs = refs
        count = packet_ref.shape[0] // sub_count
        blocks = []
        for s in range(sub_count):
            total = packet_ref[s]
            for r in range(1, count):
                total = total + packet_ref[r * sub_count + s]
            blocks.append(total)
        every = blocks[0]
        for s in range(1, sub_count):
            every = every + blocks[s]
        lane8 = iota((SUBL, LANES), 1)
        gram = []
        for total in blocks:
            gram.append(jnp.where(lane8 < n, total, 0.0))
            gram.append(jnp.where(lane8 < n, pltpu.roll(total, LANES // 2, axis=1), 0.0))
        gram = jnp.concatenate(gram, axis=0) * inverse
        pieces = -(-n0 // SUBL)
        cols = []
        for i in range(height // SUBL):
            spot = (i % 2) * (LANES // 2) + n + i // 2
            cols.append(lane_sum(jnp.where(lane8 == spot, every, 0.0)))
        first_col = jnp.concatenate(cols, axis=0) * inverse
        first_row = col_to_row(first_col, height)
        spot = n + (pieces + 1) // 2
        self_mean = sub_sum(lane_sum(jnp.where(lane8 == spot, every, 0.0))) * inverse
    else:
        gram_ref, column_ref, weights_ref = refs[:3]
        out_refs = refs[5:]
        total = packet_ref[0]
        for i in range(1, packet_ref.shape[0]):
            total = total + packet_ref[i]
        gram = gram_ref[...]
        first_row = jnp.where(lane[:1] < n, total, 0.0) * inverse
        first_col = row_to_col(first_row, height)
        self_mean = lane_sum(jnp.where(lane[:1] == LANES - 1, total, 0.0)) * inverse
    coef_col = first_col + (first_col - lane_sum(gram * first_row))
    coef_row = first_row + (first_row - sub_sum(gram * first_col))
    gram_coef = lane_sum(gram * coef_row)
    mean_square = self_mean - 2.0 * sub_sum(coef_col * first_col) + sub_sum(coef_col * gram_coef)
    norm = jnp.sqrt(mean_square + 1e-06)
    upper_half = upper_half_ref[...]
    lower_half = lower_half_ref[...]
    columns = n - 1
    shift = shift_ref[0]
    tail = lane_sum(jnp.where(lane == columns - 1, upper_half + shift * lower_half, 0.0))
    upper_coef = jnp.where(subl[:, :1] == n, norm, coef_col)
    lower_coef = tail
    weights = jnp.zeros((1, LANES), F32)
    for _ in range(2):
        projection = sub_sum(upper_half * upper_coef + lower_half * lower_coef)
        upper_coef = upper_coef - lane_sum(upper_half * projection)
        lower_coef = lower_coef - lane_sum(lower_half * projection)
        weights = weights + projection
    beta = jnp.sqrt(sub_sum(upper_coef * upper_coef + lower_coef * lower_coef) + 1e-06)
    upper_new = upper_coef / beta
    lower_new = lower_coef / beta
    upper_half = jnp.where(lane == columns, upper_new, upper_half)
    lower_half = jnp.where(lane == columns, lower_new, lower_half)
    weights = jnp.where(lane[:1] == columns, beta, weights)
    coef_wide = jnp.broadcast_to(coef_col, shape)
    if not last:
        column_ref, upper_ref, vec_ref = out_refs[:3]
        upper_half_out, lower_half_out, gram_out, weights_out, added_ref = out_refs[3:]
        added_ref[0, 0:1] = col_to_row(upper_new, height)
        added_ref[0, 1:2] = col_to_row(lower_new, height)
        upper_half_out[...] = upper_half
        lower_half_out[...] = lower_half
        weights_out[...] = jnp.broadcast_to(weights, (SUBL, LANES))
        cross_col = (first_col - gram_coef) / norm
        cross_row = (first_row - sub_sum(gram * coef_col)) / norm
        gram = jnp.where(lane == n, cross_col, gram)
        gram = jnp.where(subl == n, cross_row, gram)
        corner = jnp.logical_and(lane == n, subl == n)
        gram_out[...] = jnp.where(corner, mean_square / (norm * norm), gram)
        upper_wide = jnp.broadcast_to(upper_new, shape)
        lower_wide = jnp.broadcast_to(lower_new, shape)
        upper_last = at_sublane(upper_new, n)
        lower_last = at_sublane(lower_new, n)
        for group in range(tiles // SUBL):
            at = group * SUBL
            along, upper, lower = combine(held_ref, [coef_wide, upper_wide, lower_wide], group)
            column = (image_ref[at : at + SUBL] - along) / norm
            upper = upper + column * upper_last
            lower = lower + column * lower_last
            column_ref[at : at + SUBL] = column
            upper_ref[at : at + SUBL] = upper
            vec_ref[at : at + SUBL] = upper.astype(BF16)
            vec_ref[tiles + at : tiles + at + SUBL] = lower.astype(BF16)
    else:
        basis_ref, compact_ref, hess_ref = out_refs
        before_ref, first_ref = refs[3:5]
        out_refs = None
        old, pair, width = before_ref.shape
        compact_ref[:old, :, :width] = before_ref[...]
        compact_ref[:old, :, width:] = jnp.zeros((old, pair, n + 1 - width), F32)
        compact_ref[old : old + 1] = first_ref[:, :, : n + 1]
        compact_ref[old + 1, 0:1] = col_to_row(upper_new, height)[:, : n + 1]
        compact_ref[old + 1, 1:2] = col_to_row(lower_new, height)[:, : n + 1]
        hess_ref[0:1] = weights_ref[:1, :n]
        hess_ref[1:2] = weights[:, :n]
        coef_last = at_sublane(coef_col, n0)
        for group in range(tiles // SUBL):
            at = group * SUBL
            (along,) = combine(held_ref, [coef_wide], group)
            before = column_ref[at : at + SUBL]
            column = (image_ref[at : at + SUBL] - along - before * coef_last) / norm
            for k in range(SUBL):
                lanes = pl.ds((at + k) * LANES, LANES)
                basis_ref[0:1, lanes] = before[k : k + 1]
                basis_ref[1:2, lanes] = column[k : k + 1]


def call(body, outs, args, scratch=(), final=False, far=(), grant=GRANT, cost=None):
    specs, values = [], []
    for i, value in enumerate(args):
        space = pltpu.HBM if i in far else SM if value.shape == (1,) else VM
        specs.append(pl.BlockSpec(memory_space=space))
        values.append(
            value if space == SM else pltpu.with_memory_space_constraint(value, space)
        )
    return pl.pallas_call(
        body,
        out_shape=[
            jax.ShapeDtypeStruct(shape, dtype) if final else VM(shape, dtype)
            for shape, dtype in outs
        ],
        in_specs=specs,
        out_specs=[pl.BlockSpec(memory_space=VM)] * len(outs),
        scratch_shapes=list(scratch),
        compiler_params=pltpu.CompilerParams(vmem_limit_bytes=grant),
        cost_estimate=cost,
    )(*values)


def load(array, count, pieces, before):
    shape = (count,) + array.shape[1:]
    return call(
        functools.partial(load_kernel, pieces),
        [(shape, array.dtype)],
        [array] + before,
        [pltpu.SemaphoreType.DMA((pieces,))],
        far=(0,),
        grant=JOIN_GRANT,
        cost=pl.CostEstimate(
            flops=0,
            bytes_accessed=4 * array.size * count // array.shape[0],
            transcendentals=0,
        ),
    )[0]


def join(values, after):
    shape = (sum(value.shape[0] for value in values),) + values[0].shape[1:]
    return call(join_kernel, [(shape, values[0].dtype)], values + [after], grant=JOIN_GRANT)[0]


def window_rows(slot_map, rows_count, sub_count, tiles):
    r = lax.axis_index("rows")
    s = lax.axis_index("sub")
    half = sub_count // 2
    mine = 2
    other = mine + half - 1 + sub_count
    source = slot_map[1]
    part = source // (sub_count * tiles) - 1
    sub = (source // tiles) % sub_count
    beside = (sub ^ s) & 1
    same = sub ^ s
    within = jnp.where(
        same < 2, same, jnp.where(beside == 0, mine, other) + (same >> 1) - 1
    )
    towards = jnp.where((r + s) % 2 == 0, 1, -1)
    away = half - 1 + jnp.where(part == towards, mine + same, other + (same ^ 1))
    slice_at = jnp.where(part == 0, within, away)
    inside = (r + part >= 0) & (r + part < rows_count)
    row = jnp.where(inside, slice_at * tiles + source % tiles, -1)
    target = jnp.where(slot_map[0] >= 0, slot_map[0] ^ (s * tiles), -1)
    return row[:, None], target[None, :]


def on_device(stiffness_tiles, damping_tiles, tile_map, inv_mass, spectral_shift, basis, compact):
    rows_count = lax.axis_size("rows")
    sub_count = lax.axis_size("sub")
    devices = rows_count * sub_count
    half = sub_count // 2
    tile_size = stiffness_tiles.shape[-1]
    slots = stiffness_tiles.shape[2]
    held_count, local_rows = basis.shape
    tiles = local_rows // tile_size
    unknowns = local_rows * devices
    height = -(-held_count // (2 * SUBL)) * 2 * SUBL
    block = 2 * SUBL
    every = ("rows", "sub")

    def swap(value, partner):
        pairs = []
        for r in range(rows_count):
            for s in range(sub_count):
                to_r, to_s = partner(r, s)
                pairs.append((r * sub_count + s, to_r * sub_count + to_s))
        return lax.ppermute(value, every, pairs)

    def beside(r, s, k):
        other = r ^ 1 if s % 2 == 0 else ((r + 1) ^ 1) - 1
        if 0 <= other < rows_count:
            return other, s ^ (2 * k)
        return r, s ^ 2 if sub_count > 2 else s

    damping = damping_tiles[0, 0]
    stiffness = stiffness_tiles[0, 0]
    shift = spectral_shift.reshape(1)
    mass = inv_mass.reshape(tiles, tile_size)
    quarter = lax.axis_index("sub").reshape(1)
    source, target = window_rows(tile_map[0, 0], rows_count, sub_count, tiles)
    field = ((tiles, tile_size), F32)
    vector = ((2 * tiles, tile_size), BF16)
    square = ((height, LANES), F32)

    columns = compact.transpose(2, 0, 1)
    upper_vec, vectors, basis = call(
        start_kernel,
        [field, vector, (basis.shape, F32)],
        (columns, basis),
        [VM((2, held_count), F32), pltpu.SemaphoreType.DMA((tiles // SUBL + 1,))],
        far=(0, 1),
    )
    padding = ((0, 0), (0, height - compact.shape[1]), (0, LANES - compact.shape[2]))
    halves = jnp.pad(compact, padding)
    upper_half, lower_half = halves[0], halves[1]
    pieces = slots // block
    column = weights = added = None
    for iteration in range(ITERS):
        packed = iteration == 0
        last = iteration == ITERS - 1
        pair = jnp.stack([vectors, swap(vectors, lambda r, s: (r, s ^ 1))])
        mine = [
            swap(vectors[None], lambda r, s, k=k: (r, s ^ (2 * k))) for k in range(1, half)
        ] + [swap(pair, lambda r, s, k=k: beside(r, s, k)) for k in range(half)]
        before = [pair]
        if packed:
            _, late = lax.optimization_barrier((pair, basis))
            gram = jnp.dot(late, late.T, precision=lax.Precision.HIGHEST)
            before += [gram, source, target, upper_half, lower_half]
        loaded = load(stiffness, slots, pieces, before)
        mine = join(mine, loaded)
        other = swap(mine, lambda r, s: (r, s ^ 1))
        loaded_half = load(damping, slots // 2, pieces // 2, [mine])
        depth = tiles + SUBL if packed else tiles
        scratch = [
            VM((slots, 2 * LANES), BF16),
            VM((slots, LANES), F32),
            VM((slots // 2, tile_size, tile_size), BF16),
            pltpu.SemaphoreType.DMA((pieces // 2,)),
        ]
        args = [source, target, quarter, pair, mine, other, damping, loaded_half, loaded]
        if packed:
            args.append(gram)
            scratch.append(VM((height, LANES), F32))
        parts = call(
            functools.partial(tile_kernel, block, sub_count, packed),
            [((depth, LANES), F32)] * sub_count,
            args,
            scratch,
            far=(6,),
        )
        parts = [parts[0]] + [
            swap(parts[k], lambda r, s, k=k: (r, s ^ k)) for k in range(1, sub_count)
        ]
        packet = (devices, SUBL, LANES) if packed else (devices, 1, LANES)
        args = [shift, *parts, upper_vec, mass, basis]
        if not packed:
            args.append(column)
        image, sent = call(
            functools.partial(inner_kernel, sub_count, packed), [field, (packet, F32)], args
        )
        received = lax.all_to_all(sent, every, 0, 0)
        args = [shift, received, image, basis, upper_half, lower_half]
        if not packed:
            args += [gram, column, weights, columns, added]
        total = held_count + ITERS
        if last:
            outs = [
                ((ITERS, local_rows), F32),
                ((total - 1, 2, total), F32),
                ((ITERS, total - 1), F32),
            ]
        else:
            outs = [field, field, vector, square, square, square]
            outs += [((SUBL, LANES), F32), ((1, 2, LANES), F32)]
        outs = call(
            functools.partial(update_kernel, unknowns, sub_count, iteration, last),
            outs,
            args,
            final=last,
        )
        if not last:
            column, upper_vec, vectors, upper_half, lower_half, gram, weights, added = outs
    new_basis, compact_out, hessenberg = outs
    return new_basis, compact_out.transpose(1, 2, 0), hessenberg.T


def solution(mesh):
    in_specs = (
        P("rows", "sub", None, None, None),
        P("rows", "sub", None, None, None),
        P("rows", "sub", None, None),
        P(("rows", "sub")),
        P(),
        P(None, ("rows", "sub")),
        P(),
    )
    out_specs = (P(None, ("rows", "sub")), P(), P())
    return jax.shard_map(
        on_device, mesh=mesh, in_specs=in_specs, out_specs=out_specs, check_vma=False
    )
```

```python
import functools

import jax
import jax.numpy as jnp
from jax import lax
from jax.experimental import pallas as pl
from jax.experimental.pallas import tpu as pltpu
from jax.sharding import PartitionSpec as P

ITERS = 2
LANES = 128
SUBL = 8
F32 = jnp.float32
BF16 = jnp.bfloat16
VM = pltpu.VMEM
SM = pltpu.SMEM
GRANT = 16 * 1024 * 1024
JOIN_GRANT = 1024 * 1024
LOAD_GRANT = 8 * 1024 * 1024


def iota(shape, axis):
    return lax.broadcasted_iota(jnp.int32, shape, axis)


def lane_sum(x):
    return jnp.sum(x, axis=1, keepdims=True)


def sub_sum(x):
    return jnp.sum(x, axis=0, keepdims=True)


def row_to_col(row, height):
    shape = (height, LANES)
    return lane_sum(jnp.where(iota(shape, 0) == iota(shape, 1), row, 0.0))


def col_to_row(col, height):
    shape = (height, LANES)
    return sub_sum(jnp.where(iota(shape, 0) == iota(shape, 1), col, 0.0))


def at_sublane(col, index):
    return jnp.sum(jnp.where(iota(col.shape, 0) == index, col, 0.0), axis=0, keepdims=True)


def gather_rows(parts):
    shift = 1
    while len(parts) > 1:
        low = (iota((SUBL, LANES), 0) // shift) % 2 == 0
        merged = []
        for a, b in zip(parts[0::2], parts[1::2]):
            moved = pltpu.roll(jnp.where(low, b, a), SUBL - shift, axis=0)
            merged.append(jnp.where(low, a, b) + moved)
        parts = merged
        shift *= 2
    return parts[0]


def block_rows(held_ref):
    n = held_ref.shape[0]
    return [(i, min(SUBL, n - i)) for i in range(0, n, SUBL)]


def combine(held_ref, cols, group):
    out = []
    totals = [[] for _ in cols]
    for k in range(SUBL):
        lanes = pl.ds((group * SUBL + k) * LANES, LANES)
        sums = [None] * len(cols)
        for start, size in block_rows(held_ref):
            block = held_ref[pl.ds(start, size), lanes]
            if size < SUBL:
                block = jnp.concatenate(
                    [block, jnp.zeros((SUBL - size, LANES), F32)], axis=0
                )
            for i, col in enumerate(cols):
                term = block * col[start : start + SUBL]
                sums[i] = term if sums[i] is None else sums[i] + term
        for i in range(len(cols)):
            totals[i].append(sums[i])
    for i in range(len(cols)):
        out.append(gather_rows(totals[i]))
    return out


def start_kernel(compact_ref, basis_ref, upper_ref, vec_ref, held_ref, last_ref, sems):
    tiles = upper_ref.shape[0]
    n = held_ref.shape[0]
    groups = tiles // SUBL
    height = -(-n // SUBL) * SUBL
    span = SUBL * LANES
    first = pltpu.make_async_copy(
        compact_ref.at[compact_ref.shape[0] - 1], last_ref, sems.at[groups]
    )
    first.start()
    copies = []
    for group in range(groups):
        lanes = pl.ds(group * span, span)
        copies.append(
            pltpu.make_async_copy(basis_ref.at[:, lanes], held_ref.at[:, lanes], sems.at[group])
        )
        copies[-1].start()
    first.wait()
    rows = jnp.pad(last_ref[...], ((0, 0), (0, LANES - n)))
    cols = [
        jnp.broadcast_to(row_to_col(rows[i : i + 1], height), (height, LANES)) for i in range(2)
    ]
    for group in range(groups):
        copies[group].wait()
        upper, lower = combine(held_ref, cols, group)
        at = group * SUBL
        upper_ref[at : at + SUBL] = upper
        vec_ref[at : at + SUBL] = upper.astype(BF16)
        vec_ref[tiles + at : tiles + at + SUBL] = lower.astype(BF16)


def join_kernel(*refs):
    out_ref = refs[-1]
    at = 0
    for ref in refs[:-2]:
        out_ref[at : at + ref.shape[0]] = ref[...]
        at += ref.shape[0]


def start_copies(source_ref, start, target_ref, sems, piece):
    copies = []
    for i in range(target_ref.shape[0] // piece):
        copies.append(
            pltpu.make_async_copy(
                source_ref.at[pl.ds(start + i * piece, piece)],
                target_ref.at[pl.ds(i * piece, piece)],
                sems.at[i],
            )
        )
        copies[-1].start()
    return copies


def load_kernel(jobs, unused, *refs):
    sources, refs = refs[: len(jobs)], refs[len(jobs) + unused :]
    targets, refs = refs[: len(jobs)], refs[len(jobs) :]
    started = []
    for (start, turned, piece), source, target in zip(jobs, sources, targets):
        landing = target
        if turned:
            landing, refs = refs[0], refs[1:]
        started.append((start_copies(source, start, landing, refs[0], piece), landing))
        refs = refs[1:]
    for (_, turned, piece), target, (copies, landing) in zip(jobs, targets, started):
        for i, copy in enumerate(copies):
            copy.wait()
            if turned:
                for slot in range(i * piece, (i + 1) * piece):
                    target[slot] = landing[slot].T


def tile_kernel(
    block,
    loads,
    sub_count,
    packed,
    source_ref,
    target_ref,
    quarter_ref,
    pair_ref,
    mine_ref,
    other_ref,
    stiffness_ref,
    *rest,
):
    loaded, rest = rest[:loads], rest[loads:]
    if packed:
        gram_ref, rest = rest[0], rest[1:]
    outs, rest = rest[:sub_count], rest[sub_count:]
    picked_ref, product_ref = rest[:2]
    tiles = pair_ref.shape[1] // 2
    slots = stiffness_ref.shape[0]
    places = []
    for ref in loaded:
        places += [(ref, i) for i in range(ref.shape[0])]
    part_tiles = sub_count * tiles

    window = []
    for ref in (pair_ref, mine_ref, other_ref):
        for i in range(ref.shape[0]):
            window.append(jnp.concatenate([ref[i, :tiles], ref[i, tiles:]], axis=1))
    window = jnp.concatenate(window, axis=0)
    depth = window.shape[0]
    chooser = jnp.where(iota((slots, depth), 1) == source_ref[...], 1.0, 0.0).astype(BF16)
    picked_ref[...] = jnp.dot(chooser, window, preferred_element_type=F32).astype(BF16)

    for step in range(slots // block):
        first = step * block
        picked = picked_ref[pl.ds(first, block)]
        own = jnp.zeros((block, LANES), F32)
        for t in range(0, block, 2):
            left, right = [], []
            for slot in (first + t, first + t + 1):
                ref, i = places[slot]
                left.append(ref[i].T)
                right.append(stiffness_ref[slot])
            both = jnp.concatenate(
                [jnp.concatenate(left, axis=1), jnp.concatenate(right, axis=1)], axis=0
            )
            result = jnp.dot(picked, both, preferred_element_type=F32)
            for e in range(2):
                own = jnp.where(
                    iota((block, LANES), 0) == t + e,
                    result[:, e * LANES : (e + 1) * LANES],
                    own,
                )
        product_ref[pl.ds(first, block)] = own

    selector = jnp.where(iota((part_tiles, slots), 0) == target_ref[...], 1.0, 0.0).astype(BF16)
    left = product_ref[...]
    summed = jnp.zeros((part_tiles, LANES), F32)
    for _ in range(3):
        piece = left.astype(BF16)
        summed = summed + jnp.dot(selector, piece, preferred_element_type=F32)
        left = left - piece.astype(F32)
    for k in range(sub_count):
        outs[k][:tiles] = summed[k * tiles : (k + 1) * tiles]
    if packed:
        square_ref = rest[2]
        n = gram_ref.shape[0]
        square_ref[...] = jnp.zeros(square_ref.shape, F32)
        square_ref[:n, :n] = gram_ref[...]
        share = square_ref.shape[0] // sub_count
        for k in range(sub_count):
            start = pl.multiple_of((quarter_ref[0] ^ k) * share, SUBL)
            low = square_ref[pl.ds(start, SUBL)]
            high = square_ref[pl.ds(start + SUBL, SUBL)]
            outs[k][tiles:] = low + pltpu.roll(high, LANES // 2, axis=1)


def inner_kernel(sub_count, packed, shift_ref, *refs):
    parts = refs[:sub_count]
    upper_ref, mass_ref, held_ref = refs[sub_count : sub_count + 3]
    refs = refs[sub_count + 3 :]
    if not packed:
        column_ref, refs = refs[0], refs[1:]
    image_ref, packet_ref = refs
    tiles = upper_ref.shape[0]
    n = held_ref.shape[0]
    total = parts[0][:tiles]
    for k in range(1, sub_count):
        total = total + parts[k][:tiles]
    image = shift_ref[0] * upper_ref[...] - mass_ref[...] * total
    image_ref[...] = image
    square = lane_sum(sub_sum(image * image))
    blocks = block_rows(held_ref)
    sums = [None] * len(blocks)
    for k in range(tiles):
        row = image_ref[k : k + 1]
        for i, (start, size) in enumerate(blocks):
            term = held_ref[pl.ds(start, size), pl.ds(k * LANES, LANES)] * row
            sums[i] = term if sums[i] is None else sums[i] + term
    cols = []
    for total_block, (start, size) in zip(sums, blocks):
        col = lane_sum(total_block)
        if size < SUBL:
            col = jnp.concatenate([col, jnp.zeros((SUBL - size, 1), F32)], axis=0)
        cols.append(col)
    lane = iota((SUBL, LANES), 1)
    if packed:
        packet = parts[0][tiles:]
        for k in range(1, sub_count):
            packet = packet + parts[k][tiles:]
        for i, col in enumerate(cols):
            spot = (i % 2) * (LANES // 2) + n + i // 2
            packet = jnp.where(lane == spot, col, packet)
        spot = n + (len(cols) + 1) // 2
        first = iota((SUBL, LANES), 0) == 0
        packet = jnp.where(jnp.logical_and(lane == spot, first), square, packet)
        packet_ref[...] = jnp.broadcast_to(packet[None], packet_ref.shape)
    else:
        height = SUBL * len(cols)
        row = col_to_row(jnp.concatenate(cols, axis=0), height)
        extra = lane_sum(sub_sum(image * column_ref[...]))
        row = jnp.where(lane[:1] == n, extra, row)
        row = jnp.where(lane[:1] == LANES - 1, square, row)
        packet_ref[...] = jnp.broadcast_to(row[None], packet_ref.shape)


def update_kernel(unknowns, sub_count, iteration, last, shift_ref, *refs):
    packet_ref, image_ref, held_ref, upper_half_ref, lower_half_ref = refs[:5]
    refs = refs[5:]
    n0 = held_ref.shape[0]
    n = n0 + iteration
    tiles = image_ref.shape[0]
    height = -(-n0 // (2 * SUBL)) * 2 * SUBL
    shape = (height, LANES)
    lane = iota(shape, 1)
    subl = iota(shape, 0)
    inverse = 1.0 / unknowns
    if iteration == 0:
        out_refs = refs
        count = packet_ref.shape[0] // sub_count
        blocks = []
        for s in range(sub_count):
            total = packet_ref[s]
            for r in range(1, count):
                total = total + packet_ref[r * sub_count + s]
            blocks.append(total)
        every = blocks[0]
        for s in range(1, sub_count):
            every = every + blocks[s]
        lane8 = iota((SUBL, LANES), 1)
        gram = []
        for total in blocks:
            gram.append(jnp.where(lane8 < n, total, 0.0))
            gram.append(jnp.where(lane8 < n, pltpu.roll(total, LANES // 2, axis=1), 0.0))
        gram = jnp.concatenate(gram, axis=0) * inverse
        pieces = -(-n0 // SUBL)
        cols = []
        for i in range(height // SUBL):
            spot = (i % 2) * (LANES // 2) + n + i // 2
            cols.append(lane_sum(jnp.where(lane8 == spot, every, 0.0)))
        first_col = jnp.concatenate(cols, axis=0) * inverse
        first_row = col_to_row(first_col, height)
        spot = n + (pieces + 1) // 2
        self_mean = sub_sum(lane_sum(jnp.where(lane8 == spot, every, 0.0))) * inverse
    else:
        gram_ref, column_ref, weights_ref = refs[:3]
        out_refs = refs[5:]
        total = packet_ref[0]
        for i in range(1, packet_ref.shape[0]):
            total = total + packet_ref[i]
        gram = gram_ref[...]
        first_row = jnp.where(lane[:1] < n, total, 0.0) * inverse
        first_col = row_to_col(first_row, height)
        self_mean = lane_sum(jnp.where(lane[:1] == LANES - 1, total, 0.0)) * inverse
    coef_col = first_col + (first_col - lane_sum(gram * first_row))
    coef_row = first_row + (first_row - sub_sum(gram * first_col))
    gram_coef = lane_sum(gram * coef_row)
    mean_square = self_mean - 2.0 * sub_sum(coef_col * first_col) + sub_sum(coef_col * gram_coef)
    norm = jnp.sqrt(mean_square + 1e-06)
    upper_half = upper_half_ref[...]
    lower_half = lower_half_ref[...]
    columns = n - 1
    shift = shift_ref[0]
    tail = lane_sum(jnp.where(lane == columns - 1, upper_half + shift * lower_half, 0.0))
    upper_coef = jnp.where(subl[:, :1] == n, norm, coef_col)
    lower_coef = tail
    weights = jnp.zeros((1, LANES), F32)
    for _ in range(2):
        projection = sub_sum(upper_half * upper_coef + lower_half * lower_coef)
        upper_coef = upper_coef - lane_sum(upper_half * projection)
        lower_coef = lower_coef - lane_sum(lower_half * projection)
        weights = weights + projection
    beta = jnp.sqrt(sub_sum(upper_coef * upper_coef + lower_coef * lower_coef) + 1e-06)
    upper_new = upper_coef / beta
    lower_new = lower_coef / beta
    upper_half = jnp.where(lane == columns, upper_new, upper_half)
    lower_half = jnp.where(lane == columns, lower_new, lower_half)
    weights = jnp.where(lane[:1] == columns, beta, weights)
    coef_wide = jnp.broadcast_to(coef_col, shape)
    if not last:
        column_ref, upper_ref, vec_ref = out_refs[:3]
        upper_half_out, lower_half_out, gram_out, weights_out, added_ref = out_refs[3:]
        added_ref[0, 0:1] = col_to_row(upper_new, height)
        added_ref[0, 1:2] = col_to_row(lower_new, height)
        upper_half_out[...] = upper_half
        lower_half_out[...] = lower_half
        weights_out[...] = jnp.broadcast_to(weights, (SUBL, LANES))
        cross_col = (first_col - gram_coef) / norm
        cross_row = (first_row - sub_sum(gram * coef_col)) / norm
        gram = jnp.where(lane == n, cross_col, gram)
        gram = jnp.where(subl == n, cross_row, gram)
        corner = jnp.logical_and(lane == n, subl == n)
        gram_out[...] = jnp.where(corner, mean_square / (norm * norm), gram)
        upper_wide = jnp.broadcast_to(upper_new, shape)
        lower_wide = jnp.broadcast_to(lower_new, shape)
        upper_last = at_sublane(upper_new, n)
        lower_last = at_sublane(lower_new, n)
        for group in range(tiles // SUBL):
            at = group * SUBL
            along, upper, lower = combine(held_ref, [coef_wide, upper_wide, lower_wide], group)
            column = (image_ref[at : at + SUBL] - along) / norm
            upper = upper + column * upper_last
            lower = lower + column * lower_last
            column_ref[at : at + SUBL] = column
            upper_ref[at : at + SUBL] = upper
            vec_ref[at : at + SUBL] = upper.astype(BF16)
            vec_ref[tiles + at : tiles + at + SUBL] = lower.astype(BF16)
    else:
        basis_ref, compact_ref, hess_ref = out_refs
        before_ref, first_ref = refs[3:5]
        out_refs = None
        old, pair, width = before_ref.shape
        compact_ref[:old, :, :width] = before_ref[...]
        compact_ref[:old, :, width:] = jnp.zeros((old, pair, n + 1 - width), F32)
        compact_ref[old : old + 1] = first_ref[:, :, : n + 1]
        compact_ref[old + 1, 0:1] = col_to_row(upper_new, height)[:, : n + 1]
        compact_ref[old + 1, 1:2] = col_to_row(lower_new, height)[:, : n + 1]
        hess_ref[0:1] = weights_ref[:1, :n]
        hess_ref[1:2] = weights[:, :n]
        coef_last = at_sublane(coef_col, n0)
        for group in range(tiles // SUBL):
            at = group * SUBL
            (along,) = combine(held_ref, [coef_wide], group)
            before = column_ref[at : at + SUBL]
            column = (image_ref[at : at + SUBL] - along - before * coef_last) / norm
            for k in range(SUBL):
                lanes = pl.ds((at + k) * LANES, LANES)
                basis_ref[0:1, lanes] = before[k : k + 1]
                basis_ref[1:2, lanes] = column[k : k + 1]


def call(body, outs, args, scratch=(), final=False, far=(), grant=GRANT, cost=None):
    specs, values = [], []
    for i, value in enumerate(args):
        space = pltpu.HBM if i in far else SM if value.shape == (1,) else VM
        specs.append(pl.BlockSpec(memory_space=space))
        values.append(
            value if space == SM else pltpu.with_memory_space_constraint(value, space)
        )
    return pl.pallas_call(
        body,
        out_shape=[
            jax.ShapeDtypeStruct(shape, dtype) if final else VM(shape, dtype)
            for shape, dtype in outs
        ],
        in_specs=specs,
        out_specs=[pl.BlockSpec(memory_space=VM)] * len(outs),
        scratch_shapes=list(scratch),
        compiler_params=pltpu.CompilerParams(vmem_limit_bytes=grant),
        cost_estimate=cost,
    )(*values)


def load(jobs, before):
    outs, scratch, size = [], [], 0
    for array, start, count, turned, piece in jobs:
        assert count % piece == 0
        shape = (count,) + array.shape[1:]
        outs.append((shape, array.dtype))
        scratch += [VM(shape, array.dtype)] * turned
        scratch.append(pltpu.SemaphoreType.DMA((count // piece,)))
        size += 4 * array.size * count // array.shape[0]
    return call(
        functools.partial(
            load_kernel,
            [(start, turned, piece) for _, start, _, turned, piece in jobs],
            len(before),
        ),
        outs,
        [job[0] for job in jobs] + before,
        scratch,
        far=tuple(range(len(jobs))),
        grant=LOAD_GRANT,
        cost=pl.CostEstimate(flops=0, bytes_accessed=size, transcendentals=0),
    )


def join(values, after):
    shape = (sum(value.shape[0] for value in values),) + values[0].shape[1:]
    return call(join_kernel, [(shape, values[0].dtype)], values + [after], grant=JOIN_GRANT)[0]


def window_rows(slot_map, rows_count, sub_count, tiles):
    r = lax.axis_index("rows")
    s = lax.axis_index("sub")
    half = sub_count // 2
    mine = 2
    other = mine + half - 1 + sub_count
    source = slot_map[1]
    part = source // (sub_count * tiles) - 1
    sub = (source // tiles) % sub_count
    beside = (sub ^ s) & 1
    same = sub ^ s
    within = jnp.where(
        same < 2, same, jnp.where(beside == 0, mine, other) + (same >> 1) - 1
    )
    towards = jnp.where((r + s) % 2 == 0, 1, -1)
    away = half - 1 + jnp.where(part == towards, mine + same, other + (same ^ 1))
    slice_at = jnp.where(part == 0, within, away)
    inside = (r + part >= 0) & (r + part < rows_count)
    row = jnp.where(inside, slice_at * tiles + source % tiles, -1)
    target = jnp.where(slot_map[0] >= 0, slot_map[0] ^ (s * tiles), -1)
    return row[:, None], target[None, :]


def on_device(stiffness_tiles, damping_tiles, tile_map, inv_mass, spectral_shift, basis, compact):
    rows_count = lax.axis_size("rows")
    sub_count = lax.axis_size("sub")
    devices = rows_count * sub_count
    half = sub_count // 2
    tile_size = stiffness_tiles.shape[-1]
    slots = stiffness_tiles.shape[2]
    held_count, local_rows = basis.shape
    tiles = local_rows // tile_size
    unknowns = local_rows * devices
    height = -(-held_count // (2 * SUBL)) * 2 * SUBL
    block = 2 * SUBL
    every = ("rows", "sub")

    def swap(value, partner):
        pairs = []
        for r in range(rows_count):
            for s in range(sub_count):
                to_r, to_s = partner(r, s)
                pairs.append((r * sub_count + s, to_r * sub_count + to_s))
        return lax.ppermute(value, every, pairs)

    def beside(r, s, k):
        other = r ^ 1 if s % 2 == 0 else ((r + 1) ^ 1) - 1
        if 0 <= other < rows_count:
            return other, s ^ (2 * k)
        return r, s ^ 2 if sub_count > 2 else s

    damping = damping_tiles[0, 0]
    stiffness = stiffness_tiles[0, 0]
    shift = spectral_shift.reshape(1)
    mass = inv_mass.reshape(tiles, tile_size)
    quarter = lax.axis_index("sub").reshape(1)
    source, target = window_rows(tile_map[0, 0], rows_count, sub_count, tiles)
    field = ((tiles, tile_size), F32)
    vector = ((2 * tiles, tile_size), BF16)
    square = ((height, LANES), F32)

    columns = compact.transpose(2, 0, 1)
    upper_vec, vectors, basis = call(
        start_kernel,
        [field, vector, (basis.shape, F32)],
        (columns, basis),
        [VM((2, held_count), F32), pltpu.SemaphoreType.DMA((tiles // SUBL + 1,))],
        far=(0, 1),
    )
    padding = ((0, 0), (0, height - compact.shape[1]), (0, LANES - compact.shape[2]))
    halves = jnp.pad(compact, padding)
    upper_half, lower_half = halves[0], halves[1]
    cut = (slots * 5 // 8, slots * 3 // 8)
    column = weights = added = None
    for iteration in range(ITERS):
        packed = iteration == 0
        last = iteration == ITERS - 1
        pair = jnp.stack([vectors, swap(vectors, lambda r, s: (r, s ^ 1))])
        mine = [
            swap(vectors[None], lambda r, s, k=k: (r, s ^ (2 * k))) for k in range(1, half)
        ] + [swap(pair, lambda r, s, k=k: beside(r, s, k)) for k in range(half)]
        before = [pair]
        if packed:
            _, late = lax.optimization_barrier((pair, basis))
            gram = jnp.dot(late, late.T, precision=lax.Precision.HIGHEST)
            before += [gram, source, target, upper_half, lower_half]
        stiffness_loaded, early = load(
            [(stiffness, 0, slots, True, 2 * block), (damping, 0, cut[0], False, block)], before
        )
        mine = join(mine, early)
        other = swap(mine, lambda r, s: (r, s ^ 1))
        (middle,) = load([(damping, cut[0], cut[1], False, block)], [mine])
        depth = tiles + SUBL if packed else tiles
        scratch = [
            VM((slots, 2 * LANES), BF16),
            VM((slots, LANES), F32),
        ]
        args = [source, target, quarter, pair, mine, other, stiffness_loaded, early, middle]
        if packed:
            args.append(gram)
            scratch.append(VM((height, LANES), F32))
        parts = call(
            functools.partial(tile_kernel, block, 2, sub_count, packed),
            [((depth, LANES), F32)] * sub_count,
            args,
            scratch,
        )
        parts = [parts[0]] + [
            swap(parts[k], lambda r, s, k=k: (r, s ^ k)) for k in range(1, sub_count)
        ]
        packet = (devices, SUBL, LANES) if packed else (devices, 1, LANES)
        args = [shift, *parts, upper_vec, mass, basis]
        if not packed:
            args.append(column)
        image, sent = call(
            functools.partial(inner_kernel, sub_count, packed), [field, (packet, F32)], args
        )
        received = lax.all_to_all(sent, every, 0, 0)
        args = [shift, received, image, basis, upper_half, lower_half]
        if not packed:
            args += [gram, column, weights, columns, added]
        total = held_count + ITERS
        if last:
            outs = [
                ((ITERS, local_rows), F32),
                ((total - 1, 2, total), F32),
                ((ITERS, total - 1), F32),
            ]
        else:
            outs = [field, field, vector, square, square, square]
            outs += [((SUBL, LANES), F32), ((1, 2, LANES), F32)]
        outs = call(
            functools.partial(update_kernel, unknowns, sub_count, iteration, last),
            outs,
            args,
            final=last,
        )
        if not last:
            column, upper_vec, vectors, upper_half, lower_half, gram, weights, added = outs
    new_basis, compact_out, hessenberg = outs
    return new_basis, compact_out.transpose(1, 2, 0), hessenberg.T


def solution(mesh):
    in_specs = (
        P("rows", "sub", None, None, None),
        P("rows", "sub", None, None, None),
        P("rows", "sub", None, None),
        P(("rows", "sub")),
        P(),
        P(None, ("rows", "sub")),
        P(),
    )
    out_specs = (P(None, ("rows", "sub")), P(), P())
    return jax.shard_map(
        on_device, mesh=mesh, in_specs=in_specs, out_specs=out_specs, check_vma=False
    )
```

```python
import functools

import jax
import jax.numpy as jnp
from jax import lax
from jax.experimental import pallas as pl
from jax.experimental.pallas import tpu as pltpu
from jax.sharding import PartitionSpec as P

ITERS = 2
LANES = 128
SUBL = 8
F32 = jnp.float32
BF16 = jnp.bfloat16
VM = pltpu.VMEM
SM = pltpu.SMEM
GRANT = 16 * 1024 * 1024
JOIN_GRANT = 1024 * 1024
LOAD_GRANT = 8 * 1024 * 1024


def iota(shape, axis):
    return lax.broadcasted_iota(jnp.int32, shape, axis)


def lane_sum(x):
    return jnp.sum(x, axis=1, keepdims=True)


def sub_sum(x):
    return jnp.sum(x, axis=0, keepdims=True)


def row_to_col(row, height):
    shape = (height, LANES)
    return lane_sum(jnp.where(iota(shape, 0) == iota(shape, 1), row, 0.0))


def col_to_row(col, height):
    shape = (height, LANES)
    return sub_sum(jnp.where(iota(shape, 0) == iota(shape, 1), col, 0.0))


def at_sublane(col, index):
    return jnp.sum(jnp.where(iota(col.shape, 0) == index, col, 0.0), axis=0, keepdims=True)


def gather_rows(parts):
    shift = 1
    while len(parts) > 1:
        low = (iota((SUBL, LANES), 0) // shift) % 2 == 0
        merged = []
        for a, b in zip(parts[0::2], parts[1::2]):
            moved = pltpu.roll(jnp.where(low, b, a), SUBL - shift, axis=0)
            merged.append(jnp.where(low, a, b) + moved)
        parts = merged
        shift *= 2
    return parts[0]


def block_rows(held_ref):
    n = held_ref.shape[0]
    return [(i, min(SUBL, n - i)) for i in range(0, n, SUBL)]


def combine(held_ref, cols, group):
    out = []
    totals = [[] for _ in cols]
    for k in range(SUBL):
        lanes = pl.ds((group * SUBL + k) * LANES, LANES)
        sums = [None] * len(cols)
        for start, size in block_rows(held_ref):
            block = held_ref[pl.ds(start, size), lanes]
            if size < SUBL:
                block = jnp.concatenate(
                    [block, jnp.zeros((SUBL - size, LANES), F32)], axis=0
                )
            for i, col in enumerate(cols):
                term = block * col[start : start + SUBL]
                sums[i] = term if sums[i] is None else sums[i] + term
        for i in range(len(cols)):
            totals[i].append(sums[i])
    for i in range(len(cols)):
        out.append(gather_rows(totals[i]))
    return out


def start_kernel(compact_ref, basis_ref, upper_ref, vec_ref, held_ref, last_ref, sems):
    tiles = upper_ref.shape[0]
    n = held_ref.shape[0]
    groups = tiles // SUBL
    height = -(-n // SUBL) * SUBL
    span = SUBL * LANES
    first = pltpu.make_async_copy(
        compact_ref.at[compact_ref.shape[0] - 1], last_ref, sems.at[groups]
    )
    first.start()
    copies = []
    for group in range(groups):
        lanes = pl.ds(group * span, span)
        copies.append(
            pltpu.make_async_copy(basis_ref.at[:, lanes], held_ref.at[:, lanes], sems.at[group])
        )
        copies[-1].start()
    first.wait()
    rows = jnp.pad(last_ref[...], ((0, 0), (0, LANES - n)))
    cols = [
        jnp.broadcast_to(row_to_col(rows[i : i + 1], height), (height, LANES)) for i in range(2)
    ]
    for group in range(groups):
        copies[group].wait()
        upper, lower = combine(held_ref, cols, group)
        at = group * SUBL
        upper_ref[at : at + SUBL] = upper
        vec_ref[at : at + SUBL] = upper.astype(BF16)
        vec_ref[tiles + at : tiles + at + SUBL] = lower.astype(BF16)


def join_kernel(*refs):
    out_ref = refs[-1]
    at = 0
    for ref in refs[:-2]:
        out_ref[at : at + ref.shape[0]] = ref[...]
        at += ref.shape[0]


def start_copies(source_ref, start, target_ref, sems, piece):
    copies = []
    for i in range(target_ref.shape[0] // piece):
        copies.append(
            pltpu.make_async_copy(
                source_ref.at[pl.ds(start + i * piece, piece)],
                target_ref.at[pl.ds(i * piece, piece)],
                sems.at[i],
            )
        )
        copies[-1].start()
    return copies


def products(held_ref, span):
    n, width = held_ref.shape
    half = LANES // 2
    total = jnp.zeros((LANES, 2 * LANES), F32)
    for start in range(0, width, span):
        left = held_ref[:, start : start + span]
        left = jnp.concatenate([left, jnp.zeros((half - n, span), F32)], axis=0)
        parts = []
        for _ in range(3):
            part = left.astype(BF16)
            left = left - part.astype(F32)
            parts.append(part)
        parts.append(jnp.zeros((half, span), BF16))
        total = total + lax.dot_general(
            jnp.concatenate(parts[:2], axis=0),
            jnp.concatenate(parts, axis=0),
            (((1,), (1,)), ((), ())),
            preferred_element_type=F32,
        )
    near, far = total[:half, :LANES] + total[half:, :LANES], total[:half, LANES:]
    turned = jnp.concatenate([far, jnp.zeros((half, LANES), F32)], axis=0).T[:half]
    result = near + pltpu.roll(near, half, axis=1) + far + turned
    return jnp.where(iota(result.shape, 1) < n, result, 0.0)


def load_kernel(jobs, unused, *refs):
    sources, refs = refs[: len(jobs)], refs[len(jobs) :]
    held_ref, refs = refs[0], refs[unused:]
    targets, refs = refs[: len(jobs)], refs[len(jobs) :]
    gram_ref = None
    if len(jobs) > 1 and jobs[0][3]:
        gram_ref, refs = refs[0], refs[1:]
    started = []
    for (start, turned, piece, _), source, target in zip(jobs, sources, targets):
        landing = target
        if turned:
            landing, refs = refs[0], refs[1:]
        started.append((start_copies(source, start, landing, refs[0], piece), landing))
        refs = refs[1:]
    if gram_ref is not None:
        gram_ref[...] = products(held_ref, SUBL * LANES)
    for (_, turned, piece, _), target, (copies, landing) in zip(jobs, targets, started):
        for i, copy in enumerate(copies):
            copy.wait()
            if turned:
                for slot in range(i * piece, (i + 1) * piece):
                    target[slot] = landing[slot].T


def tile_kernel(
    block,
    loads,
    sub_count,
    packed,
    source_ref,
    target_ref,
    quarter_ref,
    pair_ref,
    mine_ref,
    other_ref,
    stiffness_ref,
    *rest,
):
    loaded, rest = rest[:loads], rest[loads:]
    if packed:
        gram_ref, rest = rest[0], rest[1:]
    outs, rest = rest[:sub_count], rest[sub_count:]
    picked_ref, product_ref = rest[:2]
    tiles = pair_ref.shape[1] // 2
    slots = stiffness_ref.shape[0]
    places = []
    for ref in loaded:
        places += [(ref, i) for i in range(ref.shape[0])]
    part_tiles = sub_count * tiles

    window = []
    for ref in (pair_ref, mine_ref, other_ref):
        for i in range(ref.shape[0]):
            window.append(jnp.concatenate([ref[i, :tiles], ref[i, tiles:]], axis=1))
    window = jnp.concatenate(window, axis=0)
    depth = window.shape[0]
    chooser = jnp.where(iota((slots, depth), 1) == source_ref[...], 1.0, 0.0).astype(BF16)
    picked_ref[...] = jnp.dot(chooser, window, preferred_element_type=F32).astype(BF16)

    for step in range(slots // block):
        first = step * block
        picked = picked_ref[pl.ds(first, block)]
        own = jnp.zeros((block, LANES), F32)
        for t in range(0, block, 2):
            left, right = [], []
            for slot in (first + t, first + t + 1):
                ref, i = places[slot]
                left.append(ref[i].T)
                right.append(stiffness_ref[slot])
            both = jnp.concatenate(
                [jnp.concatenate(left, axis=1), jnp.concatenate(right, axis=1)], axis=0
            )
            result = jnp.dot(picked, both, preferred_element_type=F32)
            for e in range(2):
                own = jnp.where(
                    iota((block, LANES), 0) == t + e,
                    result[:, e * LANES : (e + 1) * LANES],
                    own,
                )
        product_ref[pl.ds(first, block)] = own

    selector = jnp.where(iota((part_tiles, slots), 0) == target_ref[...], 1.0, 0.0).astype(BF16)
    left = product_ref[...]
    summed = jnp.zeros((part_tiles, LANES), F32)
    for _ in range(3):
        piece = left.astype(BF16)
        summed = summed + jnp.dot(selector, piece, preferred_element_type=F32)
        left = left - piece.astype(F32)
    for k in range(sub_count):
        outs[k][:tiles] = summed[k * tiles : (k + 1) * tiles]
    if packed:
        share = gram_ref.shape[0] // sub_count
        for k in range(sub_count):
            start = pl.multiple_of((quarter_ref[0] ^ k) * share, SUBL)
            low = gram_ref[pl.ds(start, SUBL)]
            high = gram_ref[pl.ds(start + SUBL, SUBL)]
            outs[k][tiles:] = low + pltpu.roll(high, LANES // 2, axis=1)


def inner_kernel(sub_count, packed, shift_ref, *refs):
    parts = refs[:sub_count]
    upper_ref, mass_ref, held_ref = refs[sub_count : sub_count + 3]
    refs = refs[sub_count + 3 :]
    if packed:
        refs = refs[2:]
    else:
        column_ref, refs = refs[0], refs[1:]
    image_ref, packet_ref = refs
    tiles = upper_ref.shape[0]
    n = held_ref.shape[0]
    total = parts[0][:tiles]
    for k in range(1, sub_count):
        total = total + parts[k][:tiles]
    image = shift_ref[0] * upper_ref[...] - mass_ref[...] * total
    image_ref[...] = image
    square = lane_sum(sub_sum(image * image))
    blocks = block_rows(held_ref)
    sums = [None] * len(blocks)
    for k in range(tiles):
        row = image_ref[k : k + 1]
        for i, (start, size) in enumerate(blocks):
            term = held_ref[pl.ds(start, size), pl.ds(k * LANES, LANES)] * row
            sums[i] = term if sums[i] is None else sums[i] + term
    cols = []
    for total_block, (start, size) in zip(sums, blocks):
        col = lane_sum(total_block)
        if size < SUBL:
            col = jnp.concatenate([col, jnp.zeros((SUBL - size, 1), F32)], axis=0)
        cols.append(col)
    lane = iota((SUBL, LANES), 1)
    if packed:
        packet = parts[0][tiles:]
        for k in range(1, sub_count):
            packet = packet + parts[k][tiles:]
        for i, col in enumerate(cols):
            spot = (i % 2) * (LANES // 2) + n + i // 2
            packet = jnp.where(lane == spot, col, packet)
        spot = n + (len(cols) + 1) // 2
        first = iota((SUBL, LANES), 0) == 0
        packet = jnp.where(jnp.logical_and(lane == spot, first), square, packet)
        packet_ref[...] = jnp.broadcast_to(packet[None], packet_ref.shape)
    else:
        height = SUBL * len(cols)
        row = col_to_row(jnp.concatenate(cols, axis=0), height)
        extra = lane_sum(sub_sum(image * column_ref[...]))
        row = jnp.where(lane[:1] == n, extra, row)
        row = jnp.where(lane[:1] == LANES - 1, square, row)
        packet_ref[...] = jnp.broadcast_to(row[None], packet_ref.shape)


def update_kernel(unknowns, sub_count, iteration, last, shift_ref, *refs):
    packet_ref, image_ref, held_ref, upper_half_ref, lower_half_ref = refs[:5]
    refs = refs[5:]
    n0 = held_ref.shape[0]
    n = n0 + iteration
    tiles = image_ref.shape[0]
    height = -(-n0 // (2 * SUBL)) * 2 * SUBL
    shape = (height, LANES)
    lane = iota(shape, 1)
    subl = iota(shape, 0)
    inverse = 1.0 / unknowns
    if iteration == 0:
        out_refs = refs
        count = packet_ref.shape[0] // sub_count
        blocks = []
        for s in range(sub_count):
            total = packet_ref[s]
            for r in range(1, count):
                total = total + packet_ref[r * sub_count + s]
            blocks.append(total)
        every = blocks[0]
        for s in range(1, sub_count):
            every = every + blocks[s]
        lane8 = iota((SUBL, LANES), 1)
        gram = []
        for total in blocks:
            gram.append(jnp.where(lane8 < n, total, 0.0))
            gram.append(jnp.where(lane8 < n, pltpu.roll(total, LANES // 2, axis=1), 0.0))
        gram = jnp.concatenate(gram, axis=0) * inverse
        pieces = -(-n0 // SUBL)
        cols = []
        for i in range(height // SUBL):
            spot = (i % 2) * (LANES // 2) + n + i // 2
            cols.append(lane_sum(jnp.where(lane8 == spot, every, 0.0)))
        first_col = jnp.concatenate(cols, axis=0) * inverse
        first_row = col_to_row(first_col, height)
        spot = n + (pieces + 1) // 2
        self_mean = sub_sum(lane_sum(jnp.where(lane8 == spot, every, 0.0))) * inverse
    else:
        gram_ref, column_ref, weights_ref = refs[:3]
        out_refs = refs[5:]
        total = packet_ref[0]
        for i in range(1, packet_ref.shape[0]):
            total = total + packet_ref[i]
        gram = gram_ref[...]
        first_row = jnp.where(lane[:1] < n, total, 0.0) * inverse
        first_col = row_to_col(first_row, height)
        self_mean = lane_sum(jnp.where(lane[:1] == LANES - 1, total, 0.0)) * inverse
    coef_col = first_col + (first_col - lane_sum(gram * first_row))
    coef_row = first_row + (first_row - sub_sum(gram * first_col))
    gram_coef = lane_sum(gram * coef_row)
    mean_square = self_mean - 2.0 * sub_sum(coef_col * first_col) + sub_sum(coef_col * gram_coef)
    norm = jnp.sqrt(mean_square + 1e-06)
    upper_half = upper_half_ref[...]
    lower_half = lower_half_ref[...]
    columns = n - 1
    shift = shift_ref[0]
    tail = lane_sum(jnp.where(lane == columns - 1, upper_half + shift * lower_half, 0.0))
    upper_coef = jnp.where(subl[:, :1] == n, norm, coef_col)
    lower_coef = tail
    weights = jnp.zeros((1, LANES), F32)
    for _ in range(2):
        projection = sub_sum(upper_half * upper_coef + lower_half * lower_coef)
        upper_coef = upper_coef - lane_sum(upper_half * projection)
        lower_coef = lower_coef - lane_sum(lower_half * projection)
        weights = weights + projection
    beta = jnp.sqrt(sub_sum(upper_coef * upper_coef + lower_coef * lower_coef) + 1e-06)
    upper_new = upper_coef / beta
    lower_new = lower_coef / beta
    upper_half = jnp.where(lane == columns, upper_new, upper_half)
    lower_half = jnp.where(lane == columns, lower_new, lower_half)
    weights = jnp.where(lane[:1] == columns, beta, weights)
    coef_wide = jnp.broadcast_to(coef_col, shape)
    if not last:
        column_ref, upper_ref, vec_ref = out_refs[:3]
        upper_half_out, lower_half_out, gram_out, weights_out, added_ref = out_refs[3:]
        added_ref[0, 0:1] = col_to_row(upper_new, height)
        added_ref[0, 1:2] = col_to_row(lower_new, height)
        upper_half_out[...] = upper_half
        lower_half_out[...] = lower_half
        weights_out[...] = jnp.broadcast_to(weights, (SUBL, LANES))
        cross_col = (first_col - gram_coef) / norm
        cross_row = (first_row - sub_sum(gram * coef_col)) / norm
        gram = jnp.where(lane == n, cross_col, gram)
        gram = jnp.where(subl == n, cross_row, gram)
        corner = jnp.logical_and(lane == n, subl == n)
        gram_out[...] = jnp.where(corner, mean_square / (norm * norm), gram)
        upper_wide = jnp.broadcast_to(upper_new, shape)
        lower_wide = jnp.broadcast_to(lower_new, shape)
        upper_last = at_sublane(upper_new, n)
        lower_last = at_sublane(lower_new, n)
        for group in range(tiles // SUBL):
            at = group * SUBL
            along, upper, lower = combine(held_ref, [coef_wide, upper_wide, lower_wide], group)
            column = (image_ref[at : at + SUBL] - along) / norm
            upper = upper + column * upper_last
            lower = lower + column * lower_last
            column_ref[at : at + SUBL] = column
            upper_ref[at : at + SUBL] = upper
            vec_ref[at : at + SUBL] = upper.astype(BF16)
            vec_ref[tiles + at : tiles + at + SUBL] = lower.astype(BF16)
    else:
        basis_ref, compact_ref, hess_ref = out_refs
        before_ref, first_ref = refs[3:5]
        out_refs = None
        old, pair, width = before_ref.shape
        compact_ref[:old, :, :width] = before_ref[...]
        compact_ref[:old, :, width:] = jnp.zeros((old, pair, n + 1 - width), F32)
        compact_ref[old : old + 1] = first_ref[:, :, : n + 1]
        compact_ref[old + 1, 0:1] = col_to_row(upper_new, height)[:, : n + 1]
        compact_ref[old + 1, 1:2] = col_to_row(lower_new, height)[:, : n + 1]
        hess_ref[0:1] = weights_ref[:1, :n]
        hess_ref[1:2] = weights[:, :n]
        coef_last = at_sublane(coef_col, n0)
        for group in range(tiles // SUBL):
            at = group * SUBL
            (along,) = combine(held_ref, [coef_wide], group)
            before = column_ref[at : at + SUBL]
            column = (image_ref[at : at + SUBL] - along - before * coef_last) / norm
            for k in range(SUBL):
                lanes = pl.ds((at + k) * LANES, LANES)
                basis_ref[0:1, lanes] = before[k : k + 1]
                basis_ref[1:2, lanes] = column[k : k + 1]


def call(body, outs, args, scratch=(), final=False, far=(), grant=GRANT, cost=None):
    specs, values = [], []
    for i, value in enumerate(args):
        space = pltpu.HBM if i in far else SM if value.shape == (1,) else VM
        specs.append(pl.BlockSpec(memory_space=space))
        values.append(
            value if space == SM else pltpu.with_memory_space_constraint(value, space)
        )
    return pl.pallas_call(
        body,
        out_shape=[
            jax.ShapeDtypeStruct(shape, dtype) if final else VM(shape, dtype)
            for shape, dtype in outs
        ],
        in_specs=specs,
        out_specs=[pl.BlockSpec(memory_space=VM)] * len(outs),
        scratch_shapes=list(scratch),
        compiler_params=pltpu.CompilerParams(vmem_limit_bytes=grant),
        cost_estimate=cost,
    )(*values)


def load(jobs, before, gram=False):
    outs, scratch, size = [], [], 0
    for array, start, count, turned, piece in jobs:
        assert count % piece == 0
        shape = (count,) + array.shape[1:]
        outs.append((shape, array.dtype))
        scratch += [VM(shape, array.dtype)] * turned
        scratch.append(pltpu.SemaphoreType.DMA((count // piece,)))
        size += 4 * array.size * count // array.shape[0]
    if gram:
        outs.append(((LANES // 2, LANES), F32))
    return call(
        functools.partial(
            load_kernel,
            [(start, turned, piece, gram) for _, start, _, turned, piece in jobs],
            len(before),
        ),
        outs,
        [job[0] for job in jobs] + before,
        scratch,
        far=tuple(range(len(jobs))),
        grant=LOAD_GRANT,
        cost=pl.CostEstimate(flops=0, bytes_accessed=size, transcendentals=0),
    )


def join(values, after):
    shape = (sum(value.shape[0] for value in values),) + values[0].shape[1:]
    return call(join_kernel, [(shape, values[0].dtype)], values + [after], grant=JOIN_GRANT)[0]


def window_rows(slot_map, rows_count, sub_count, tiles):
    r = lax.axis_index("rows")
    s = lax.axis_index("sub")
    half = sub_count // 2
    mine = 2
    other = mine + half - 1 + sub_count
    source = slot_map[1]
    part = source // (sub_count * tiles) - 1
    sub = (source // tiles) % sub_count
    beside = (sub ^ s) & 1
    same = sub ^ s
    within = jnp.where(
        same < 2, same, jnp.where(beside == 0, mine, other) + (same >> 1) - 1
    )
    towards = jnp.where((r + s) % 2 == 0, 1, -1)
    away = half - 1 + jnp.where(part == towards, mine + same, other + (same ^ 1))
    slice_at = jnp.where(part == 0, within, away)
    inside = (r + part >= 0) & (r + part < rows_count)
    row = jnp.where(inside, slice_at * tiles + source % tiles, -1)
    target = jnp.where(slot_map[0] >= 0, slot_map[0] ^ (s * tiles), -1)
    return row[:, None], target[None, :]


def on_device(stiffness_tiles, damping_tiles, tile_map, inv_mass, spectral_shift, basis, compact):
    rows_count = lax.axis_size("rows")
    sub_count = lax.axis_size("sub")
    devices = rows_count * sub_count
    half = sub_count // 2
    tile_size = stiffness_tiles.shape[-1]
    slots = stiffness_tiles.shape[2]
    held_count, local_rows = basis.shape
    tiles = local_rows // tile_size
    unknowns = local_rows * devices
    height = -(-held_count // (2 * SUBL)) * 2 * SUBL
    block = 2 * SUBL
    every = ("rows", "sub")

    def swap(value, partner):
        pairs = []
        for r in range(rows_count):
            for s in range(sub_count):
                to_r, to_s = partner(r, s)
                pairs.append((r * sub_count + s, to_r * sub_count + to_s))
        return lax.ppermute(value, every, pairs)

    def beside(r, s, k):
        other = r ^ 1 if s % 2 == 0 else ((r + 1) ^ 1) - 1
        if 0 <= other < rows_count:
            return other, s ^ (2 * k)
        return r, s ^ 2 if sub_count > 2 else s

    damping = damping_tiles[0, 0]
    stiffness = stiffness_tiles[0, 0]
    shift = spectral_shift.reshape(1)
    mass = inv_mass.reshape(tiles, tile_size)
    quarter = lax.axis_index("sub").reshape(1)
    field = ((tiles, tile_size), F32)
    vector = ((2 * tiles, tile_size), BF16)
    square = ((height, LANES), F32)

    columns = compact.transpose(2, 0, 1)
    upper_vec, vectors, basis = call(
        start_kernel,
        [field, vector, (basis.shape, F32)],
        (columns, basis),
        [VM((2, held_count), F32), pltpu.SemaphoreType.DMA((tiles // SUBL + 1,))],
        far=(0, 1),
    )
    cut = (slots // 2, slots // 2)
    column = weights = added = None
    for iteration in range(ITERS):
        packed = iteration == 0
        last = iteration == ITERS - 1
        pair = jnp.stack([vectors, swap(vectors, lambda r, s: (r, s ^ 1))])
        mine = [
            swap(vectors[None], lambda r, s, k=k: (r, s ^ (2 * k))) for k in range(1, half)
        ] + [swap(pair, lambda r, s, k=k: beside(r, s, k)) for k in range(half)]
        before = [pair]
        if packed:
            _, late_map = lax.optimization_barrier((pair, tile_map))
            source, target = window_rows(late_map[0, 0], rows_count, sub_count, tiles)
            before = [basis, pair, source, target, shift]
        stiffness_loaded, early, *products_here = load(
            [
                (stiffness, 0, slots, True, 2 * block),
                (damping, 0, cut[0], False, block),
            ],
            before,
            packed,
        )
        if packed:
            (gram,) = products_here
        mine = join(mine, early)
        other = swap(mine, lambda r, s: (r, s ^ 1))
        (middle,) = load([(damping, cut[0], cut[1], False, block)], [mine])
        depth = tiles + SUBL if packed else tiles
        scratch = [
            VM((slots, 2 * LANES), BF16),
            VM((slots, LANES), F32),
        ]
        args = [source, target, quarter, pair, mine, other, stiffness_loaded, early, middle]
        if packed:
            args.append(gram)
        parts = call(
            functools.partial(tile_kernel, block, 2, sub_count, packed),
            [((depth, LANES), F32)] * sub_count,
            args,
            scratch,
        )
        parts = [parts[0]] + [
            swap(parts[k], lambda r, s, k=k: (r, s ^ k)) for k in range(1, sub_count)
        ]
        if packed:
            _, late = lax.optimization_barrier((parts[0], compact))
            padding = ((0, 0), (0, height - late.shape[1]), (0, LANES - late.shape[2]))
            halves = jnp.pad(late, padding)
            upper_half, lower_half = halves[0], halves[1]
        packet = (devices, SUBL, LANES) if packed else (devices, 1, LANES)
        args = [shift, *parts, upper_vec, mass, basis]
        args += [upper_half, lower_half] if packed else [column]
        image, sent = call(
            functools.partial(inner_kernel, sub_count, packed), [field, (packet, F32)], args
        )
        received = lax.all_to_all(sent, every, 0, 0)
        args = [shift, received, image, basis, upper_half, lower_half]
        if not packed:
            args += [gram, column, weights, columns, added]
        total = held_count + ITERS
        if last:
            outs = [
                ((ITERS, local_rows), F32),
                ((total - 1, 2, total), F32),
                ((ITERS, total - 1), F32),
            ]
        else:
            outs = [field, field, vector, square, square, square]
            outs += [((SUBL, LANES), F32), ((1, 2, LANES), F32)]
        outs = call(
            functools.partial(update_kernel, unknowns, sub_count, iteration, last),
            outs,
            args,
            final=last,
        )
        if not last:
            column, upper_vec, vectors, upper_half, lower_half, gram, weights, added = outs
    new_basis, compact_out, hessenberg = outs
    return new_basis, compact_out.transpose(1, 2, 0), hessenberg.T


def solution(mesh):
    in_specs = (
        P("rows", "sub", None, None, None),
        P("rows", "sub", None, None, None),
        P("rows", "sub", None, None),
        P(("rows", "sub")),
        P(),
        P(None, ("rows", "sub")),
        P(),
    )
    out_specs = (P(None, ("rows", "sub")), P(), P())
    return jax.shard_map(
        on_device, mesh=mesh, in_specs=in_specs, out_specs=out_specs, check_vma=False
    )
```
